512 devices in a mesh: expert: 32 (over z, core), dp: 16 (over x, y).
Axes of the slice: x: 4, y: 4, z: 16, core: 2. Of those that a mesh axis runs over, the one named last changes fastest.
Arguments:
- patches: bfloat16 [16, 32, 128, 1664], P('dp', 'expert'), may hold values from -6 to 6
- grad_out: bfloat16 [16, 32, 128, 1664], P('dp', 'expert'), may hold values from -3 to 3
- weight_in: bfloat16 [32, 1664, 4096], P('expert', None, 'dp'), may hold values from -0.15625 to 0.15625
- weight_out: bfloat16 [32, 4096, 1664], P('expert', 'dp'), may hold values from -0.09375 to 0.09375
- gates: float32 [32, 16, 32], P('expert', 'dp'), may hold values from 0.1 to 1
- counts: int32 [16, 32, 32], P(None, None, 'expert'), may hold values from 0 to 2, as said below
- picks: int32 [16, 32, 32, 2], P('dp', 'expert'), may hold values from 0 to 127, as said below
Outputs:
- grad_patches: bfloat16 [16, 32, 128, 1664], P('dp', 'expert')
- grad_weight_in: bfloat16 [32, 1664, 4096], P('expert', None, 'dp')
- grad_weight_out: bfloat16 [32, 4096, 1664], P('expert', 'dp')
The draws below stay inside these ranges and needn't reach their ends.
Inputs may be any that keep to these rules, and one draw needn't show every extreme that they name: For each group and expert the counts over the 32 owner blocks sum to exactly 32, and in every group each expert takes 2 patches from some owner block. `picks`: for each group, owner block and expert the entries are distinct; only the first counts[g, o, e] of them are taken, the rest are arbitrary patch indices of the block.
All inputs are finite; a program needn't handle non-finite values.
Results may differ from the reference program's by a relative error of at most 0.015.
Values may be sent and summed in bfloat16 or wider, within the bound.
A program may use at most 64 MiB of HBM per device.

```python
import jax
import jax.numpy as jnp
from jax import lax

D = 1664
FF = 4096
MOST = 2
TOK_DEV = 128
EXPERTS = 32
OWNERS = 32
GROUPS = 16
CAP = 32
N_DP = 16


def draw_counts(key, part):
    slot_total = OWNERS * MOST
    scores = jax.random.randint(jax.random.fold_in(key, 11), (GROUPS, EXPERTS, slot_total), 0, 2 ** 20)
    favored = jax.random.randint(jax.random.fold_in(key, 12), (GROUPS, EXPERTS, 1), 0, OWNERS)
    slot_owner = jnp.arange(slot_total, dtype=jnp.int32) // MOST
    scores = scores * slot_total + jnp.arange(slot_total, dtype=jnp.int32) + jnp.where(slot_owner == favored, 2 ** 28, 0)
    taken_slots = lax.top_k(scores, CAP)[1]
    owner_hits = taken_slots[..., None] // MOST == jnp.arange(OWNERS, dtype=jnp.int32)
    per_owner = jnp.sum(owner_hits.astype(jnp.int32), axis=2)
    return jnp.transpose(per_owner, (0, 2, 1)).astype(jnp.int32)


def draw_picks(key, part):
    scores = jax.random.randint(jax.random.fold_in(key, 21), (GROUPS, OWNERS, EXPERTS, TOK_DEV), 0, 2 ** 20)
    scores = scores * TOK_DEV + jnp.arange(TOK_DEV, dtype=jnp.int32)
    return lax.top_k(scores, MOST)[1].astype(jnp.int32)


def steps_of(stream_key, extent, split, low, high):
    gain = 1.0
    for dim, shards_of in split:
        heights = jax.random.uniform(jax.random.fold_in(jax.random.fold_in(stream_key, 6), dim), (shards_of,), jnp.float32, low / len(split), high / len(split))
        gain = gain * jnp.repeat(jnp.exp(heights), extent[dim] // shards_of).reshape((-1,) + (1,) * (len(extent) - 1 - dim))
    return gain


def bell_draw(key, shape, deviation, bound, pieces=(), kind=jnp.bfloat16):
    array = jax.random.normal(key, shape, jnp.float32) * deviation
    if len(pieces) > 0:
        array = steps_of(key, shape, pieces, -0.22, 0.18) * array
    return jnp.clip(array, min=-bound, max=bound).astype(kind)


def setup_inputs(seed: int = 0) -> dict:
    streams_of = jax.random.split(jax.random.key(seed), 8)
    return {
        "patches": bell_draw(streams_of[0], (GROUPS, OWNERS, TOK_DEV, D), 1.0, 6.0, ((0, 16), (1, 32))),
        "grad_out": bell_draw(streams_of[1], (GROUPS, OWNERS, TOK_DEV, D), 0.5, 3.0, ((0, 16), (1, 32))),
        "weight_in": bell_draw(streams_of[2], (EXPERTS, D, FF), D ** -0.5, 0.15625, ((0, 32), (2, 16))),
        "weight_out": bell_draw(streams_of[3], (EXPERTS, FF, D), FF ** -0.5, 0.09375, ((0, 32), (1, 16))),
        "gates": jnp.clip(0.1 + 0.9 * jax.random.uniform(streams_of[4], (EXPERTS, GROUPS, CAP), jnp.float32) ** steps_of(streams_of[4], (EXPERTS, GROUPS, CAP), ((0, 32), (1, 16)), -0.2, 0.2), 0.1, 1.0),
        "counts": draw_counts(jax.random.fold_in(streams_of[7], 71), 0),
        "picks": draw_picks(jax.random.fold_in(streams_of[7], 71), 0),
    }


gelu_scale = 0.7978845608028654
gelu_cubic = 0.044715


def gelu_parts(preact):
    inner_arg = gelu_scale * (preact + gelu_cubic * preact * preact * preact)
    tangent = jnp.tanh(inner_arg)
    gelu_value = 0.5 * preact * (1.0 + tangent)
    gelu_slope = 0.5 * (1.0 + tangent) + 0.5 * preact * (1.0 - tangent * tangent) * gelu_scale * (1.0 + 3.0 * gelu_cubic * preact * preact)
    return gelu_value, gelu_slope


def slot_tables(owner_counts, capacity):
    owners = owner_counts.shape[-1]
    slot_ends = jnp.cumsum(owner_counts, axis=-1).astype(jnp.int32)
    begins = (slot_ends - owner_counts).astype(jnp.int32)
    slot_ids = jnp.arange(capacity, dtype=jnp.int32)
    owner_of = jnp.sum((slot_ends[..., None, :] <= slot_ids[:, None]).astype(jnp.int32), axis=-1).astype(jnp.int32)
    matches = owner_of[..., None] == jnp.arange(owners, dtype=jnp.int32)
    rank_in = (slot_ids - jnp.sum(jnp.where(matches, begins[..., None, :], 0), axis=-1)).astype(jnp.int32)
    return owner_of, rank_in


def reference(patches, grad_out, weight_in, weight_out, gates, counts, picks):
    groups = patches.shape[0]
    dim_model = patches.shape[3]
    group_ids = jnp.arange(groups, dtype=jnp.int32)[:, None]

    def one_expert(grad_acc, expert):
        owner_of, rank_in = slot_tables(counts[:, :, expert], CAP)
        picked = picks[:, :, expert, :]
        patch_ids = picked[group_ids, owner_of, rank_in].astype(jnp.int32)
        expert_in = patches[group_ids, owner_of, patch_ids].reshape(groups * CAP, dim_model)
        chosen_grad = grad_out[group_ids, owner_of, patch_ids]
        scaled = (gates[expert][:, :, None] * chosen_grad.astype(jnp.float32)).astype(jnp.bfloat16)
        scaled = scaled.reshape(groups * CAP, dim_model)
        local_in = weight_in[expert]
        local_out = weight_out[expert]
        preact = jnp.dot(expert_in, local_in, preferred_element_type=jnp.float32)
        gelu_value, gelu_slope = gelu_parts(preact)
        hidden = gelu_value.astype(jnp.bfloat16)
        grad_hidden = jnp.dot(scaled, local_out.T, preferred_element_type=jnp.float32)
        grad_pre = (grad_hidden * gelu_slope).astype(jnp.bfloat16)
        grad_w_out = jnp.dot(hidden.T, scaled, preferred_element_type=jnp.float32).astype(jnp.bfloat16)
        grad_w_in = jnp.dot(expert_in.T, grad_pre, preferred_element_type=jnp.float32).astype(jnp.bfloat16)
        pre_blocks = grad_pre.astype(jnp.float32).reshape(groups * CAP, N_DP, FF // N_DP)
        in_blocks = local_in.astype(jnp.float32).reshape(dim_model, N_DP, FF // N_DP)
        partial_value = jnp.einsum("rkf,dkf->krd", pre_blocks, in_blocks).astype(jnp.bfloat16)
        expert_grad = jnp.sum(partial_value.astype(jnp.float32), axis=0).astype(jnp.bfloat16)
        expert_grad = expert_grad.reshape(groups, CAP, dim_model).astype(jnp.float32)
        grad_acc = grad_acc.at[group_ids, owner_of, patch_ids].add(expert_grad)
        return grad_acc, (grad_w_in, grad_w_out)

    initial = jnp.zeros(patches.shape, jnp.float32)
    grad_acc, stacked = lax.scan(one_expert, initial, jnp.arange(EXPERTS, dtype=jnp.int32))
    return (grad_acc.astype(jnp.bfloat16), stacked[0], stacked[1])
```

```python
import functools

import jax
import jax.numpy as jnp
from jax import lax
from jax.experimental import pallas as pl
from jax.experimental.pallas import tpu as pltpu
from jax.sharding import PartitionSpec as P

MESH = pl.DeviceIdType.MESH
SIDE = 4
HALF = 16

gelu_scale = 0.7978845608028654
gelu_cubic = 0.044715


def gelu_parts(preact):
    inner_arg = gelu_scale * (preact + gelu_cubic * preact * preact * preact)
    tangent = jnp.tanh(inner_arg)
    gelu_value = 0.5 * preact * (1.0 + tangent)
    gelu_slope = 0.5 * (1.0 + tangent) + 0.5 * preact * (1.0 - tangent * tangent) * gelu_scale * (
        1.0 + 3.0 * gelu_cubic * preact * preact
    )
    return (gelu_value, gelu_slope)


def meet(axis, peers):
    barrier = pltpu.get_barrier_semaphore()
    for peer in peers:
        pl.semaphore_signal(barrier, inc=1, device_id={axis: peer}, device_id_type=MESH)
    pl.semaphore_wait(barrier, len(peers))


def exchange_kernel(count, size, *refs):
    sources, targets = refs[:count], refs[count : 2 * count]
    send_sem, recv_sem, own_sem = refs[2 * count :]
    me = lax.axis_index("expert")
    barrier = pltpu.get_barrier_semaphore()

    def offset_of(step):
        sign = 1 - 2 * lax.rem(step, 2)
        return size // 2 + sign * lax.div(step + 1, 2)

    def greet(step, carry):
        peer = lax.rem(me + offset_of(step), size)
        pl.semaphore_signal(barrier, inc=1, device_id={"expert": peer}, device_id_type=MESH)
        return carry

    lax.fori_loop(0, size - 1, greet, 0)
    own = [
        pltpu.make_async_copy(sources[i].at[me], targets[i].at[me], own_sem.at[i])
        for i in range(count)
    ]
    for copy in own:
        copy.start()
    pl.semaphore_wait(barrier, size - 1)

    def outgoing(i, step):
        offset = offset_of(step)
        peer = lax.rem(me + offset, size)
        return pltpu.make_async_remote_copy(
            src_ref=sources[i].at[peer],
            dst_ref=targets[i].at[me],
            send_sem=send_sem.at[i, offset],
            recv_sem=recv_sem.at[i, offset],
            device_id={"expert": peer},
            device_id_type=MESH,
        )

    def incoming(i, step):
        offset = offset_of(step)
        peer = lax.rem(me + size - offset, size)
        return pltpu.make_async_remote_copy(
            src_ref=sources[i].at[peer],
            dst_ref=targets[i].at[peer],
            send_sem=send_sem.at[i, offset],
            recv_sem=recv_sem.at[i, offset],
            device_id={"expert": peer},
            device_id_type=MESH,
        )

    for i in range(count):

        def launch(step, carry, i=i):
            outgoing(i, step).start()
            return carry

        lax.fori_loop(0, size - 1, launch, 0)
    for i in range(count):

        def finish(step, carry, i=i):
            incoming(i, step).wait_recv()
            outgoing(i, step).wait_send()
            return carry

        lax.fori_loop(0, size - 1, finish, 0)
    for copy in own:
        copy.wait()


def exchange(collective_id, *arrays):
    size = arrays[0].shape[0]
    count = len(arrays)
    in_vmem = pl.BlockSpec(memory_space=pltpu.VMEM)
    return pl.pallas_call(
        functools.partial(exchange_kernel, count, size),
        out_shape=[jax.ShapeDtypeStruct(a.shape, a.dtype) for a in arrays],
        in_specs=[in_vmem] * count,
        out_specs=[in_vmem] * count,
        scratch_shapes=[
            pltpu.SemaphoreType.DMA((count, size)),
            pltpu.SemaphoreType.DMA((count, size)),
            pltpu.SemaphoreType.DMA((count,)),
        ],
        compiler_params=pltpu.CompilerParams(collective_id=collective_id, has_side_effects=True),
    )(*arrays)


def wrap(value):
    return lax.rem(value + 2 * SIDE, SIDE)


def place(half, first, second):
    return first * SIDE + second if half == 0 else second * SIDE + first


def spread_kernel(in_ref, grad_ref, in_all, grad_all, send_sem, recv_sem, own_sem):
    me = lax.axis_index("dp")
    spot_x, spot_y = lax.div(me, SIDE), lax.rem(me, SIDE)
    inputs, outputs = (in_ref, grad_ref), (in_all, grad_all)
    own = [pltpu.make_async_copy(inputs[i], outputs[i].at[me], own_sem.at[i]) for i in range(2)]
    for copy in own:
        copy.start()
    meet(
        "dp",
        [
            place(0, wrap(spot_x + 1), spot_y),
            place(0, wrap(spot_x - 1), spot_y),
            place(0, spot_x, wrap(spot_y + 1)),
            place(0, spot_x, wrap(spot_y - 1)),
        ],
    )
    shifts = (0, -1, 1, 2)
    moves = ((0, 1), (1, 1), (0, -1), (1, -1), (0, 1), (1, -1))

    def piece(half, stage, move, incoming):
        which, way = moves[move]
        first, second = (spot_x, spot_y) if half == 0 else (spot_y, spot_x)
        rows = pl.ds(half * HALF, HALF)
        back = (0 if move < 4 else -way) - (way if incoming else 0)
        if stage == 0:
            block = place(half, wrap(first + back), second)
            peer = place(half, wrap(first + way), second)
        else:
            held = wrap(first + shifts[stage - 1])
            block = place(half, held, wrap(second + back))
            peer = place(half, first, wrap(second + way))
        target = outputs[which].at[block, rows, :]
        source = target
        if not incoming and move < 4 and stage < 2:
            source = inputs[which].at[rows, :]
        return pltpu.make_async_remote_copy(
            src_ref=source,
            dst_ref=target,
            send_sem=send_sem.at[half, stage, move],
            recv_sem=recv_sem.at[half, stage, move],
            device_id={"dp": peer},
            device_id_type=MESH,
        )

    def launch(half, stage, move):
        piece(half, stage, move, False).start()

    def arrive(half, stage, move):
        piece(half, stage, move, True).wait_recv()

    def relay(half, stage):
        arrive(half, stage, 0)
        launch(half, stage, 4)
        arrive(half, stage, 3)
        launch(half, stage, 5)

    halves = range(2)
    for stage in (0, 1):
        for move in range(4):
            for half in halves:
                launch(half, stage, move)
    for half in halves:
        relay(half, 0)
    for half in halves:
        arrive(half, 0, 1)
        for move in range(4):
            launch(half, 2, move)
    for half in halves:
        arrive(half, 0, 2)
        for move in range(4):
            launch(half, 3, move)
    for half in halves:
        relay(half, 1)
    for half in halves:
        arrive(half, 0, 4)
        arrive(half, 0, 5)
        for move in range(4):
            launch(half, 4, move)
    for stage in (2, 3, 4):
        for half in halves:
            relay(half, stage)
    for stage in (1, 2, 3, 4):
        for half in halves:
            for move in (1, 2, 4, 5):
                arrive(half, stage, move)
    for stage in range(5):
        for half in halves:
            for move in range(6):
                piece(half, stage, move, False).wait_send()
    for copy in own:
        copy.wait()


def spread(collective_id, rows_in, rows_grad):
    in_vmem = pl.BlockSpec(memory_space=pltpu.VMEM)
    whole = jax.ShapeDtypeStruct((SIDE * SIDE,) + rows_in.shape, rows_in.dtype)
    return pl.pallas_call(
        spread_kernel,
        out_shape=[whole, whole],
        in_specs=[in_vmem] * 2,
        out_specs=[in_vmem] * 2,
        scratch_shapes=[
            pltpu.SemaphoreType.DMA((2, 5, 6)),
            pltpu.SemaphoreType.DMA((2, 5, 6)),
            pltpu.SemaphoreType.DMA((2,)),
        ],
        compiler_params=pltpu.CompilerParams(collective_id=collective_id, has_side_effects=True),
    )(rows_in, rows_grad)


def collect_kernel(parts, total, near, passing, summed, last, send_sem, recv_sem):
    me = lax.axis_index("dp")
    spot_x, spot_y = lax.div(me, SIDE), lax.rem(me, SIDE)
    meet(
        "dp",
        [place(0, wrap(spot_x + shift), spot_y) for shift in (1, -1, 2)]
        + [place(0, spot_x, wrap(spot_y + shift)) for shift in (1, -1, 2)],
    )

    def unit(half, spot, begin=0, count=SIDE):
        rows = pl.ds(half * HALF, HALF)
        if half == 0:
            return parts.at[spot, pl.ds(begin, count), rows, :]
        return parts.at[pl.ds(begin, count), spot, rows, :]

    def piece(half, move):
        first, second = (spot_x, spot_y) if half == 0 else (spot_y, spot_x)
        if move == 0:
            way, source, target = 1, unit(half, wrap(first + 1)), near.at[half, 0]
        elif move == 1:
            way, source, target = -1, unit(half, wrap(first - 1)), near.at[half, 1]
        elif move == 2:
            way, source, target = 1, unit(half, wrap(first + 2), 0, 2), passing.at[half, 0]
        elif move == 3:
            way, source, target = -1, unit(half, wrap(first + 2), 2, 2), passing.at[half, 1]
        elif move == 4:
            way, source, target = 1, passing.at[half, 0], near.at[half, 2, pl.ds(0, 2)]
        elif move == 5:
            way, source, target = -1, passing.at[half, 1], near.at[half, 2, pl.ds(2, 2)]
        else:
            way = (1, -1, 2)[move - 6]
            source, target = summed.at[half, wrap(second + way)], last.at[half, move - 6]
        if move < 6:
            peer = place(half, wrap(first + way), second)
        else:
            peer = place(half, first, wrap(second + way))
        return pltpu.make_async_remote_copy(
            src_ref=source,
            dst_ref=target,
            send_sem=send_sem.at[half, move],
            recv_sem=recv_sem.at[half, move],
            device_id={"dp": peer},
            device_id_type=MESH,
        )

    halves = range(2)
    for move in (2, 3, 0, 1):
        for half in halves:
            piece(half, move).start()
    for half in halves:
        piece(half, 2).wait_recv()
        piece(half, 4).start()
        piece(half, 3).wait_recv()
        piece(half, 5).start()
    for half in halves:
        for move in (0, 1, 4, 5):
            piece(half, move).wait_recv()
        mine = spot_x if half == 0 else spot_y
        for spot in range(SIDE):
            rows = slice(half * HALF, half * HALF + HALF)
            own = parts[mine, spot, rows, :] if half == 0 else parts[spot, mine, rows, :]
            value = own.astype(jnp.float32)
            for source in range(3):
                value = value + near[half, source, spot].astype(jnp.float32)
            summed[half, spot] = value.astype(summed.dtype)
        for move in (8, 6, 7):
            piece(half, move).start()
    for half in halves:
        for move in (6, 7, 8):
            piece(half, move).wait_recv()
        mine = spot_y if half == 0 else spot_x
        value = summed[half, mine].astype(jnp.float32)
        for source in range(3):
            value = value + last[half, source].astype(jnp.float32)
        total[half * HALF : half * HALF + HALF, :] = value.astype(total.dtype)
    for half in halves:
        for move in range(9):
            piece(half, move).wait_send()


def collect(collective_id, parts):
    rows, width = parts.shape[2:]
    in_vmem = pl.BlockSpec(memory_space=pltpu.VMEM)
    kind = parts.dtype
    return pl.pallas_call(
        collect_kernel,
        out_shape=jax.ShapeDtypeStruct((rows, width), kind),
        in_specs=[in_vmem],
        out_specs=in_vmem,
        scratch_shapes=[
            pltpu.VMEM((2, 3, SIDE, HALF, width), kind),
            pltpu.VMEM((2, 2, 2, HALF, width), kind),
            pltpu.VMEM((2, SIDE, HALF, width), kind),
            pltpu.VMEM((2, 3, HALF, width), kind),
            pltpu.SemaphoreType.DMA((2, 9)),
            pltpu.SemaphoreType.DMA((2, 9)),
        ],
        compiler_params=pltpu.CompilerParams(collective_id=collective_id, has_side_effects=True),
    )(parts)


def on_device(patches, grad_out, weight_in, weight_out, gates, counts, picks):
    tok_local = patches.shape[2]
    dim_model = patches.shape[3]
    experts = picks.shape[2]
    per_owner = picks.shape[3]
    groups = counts.shape[0]
    owners = counts.shape[1]
    capacity = gates.shape[2]
    local_in = weight_in[0]
    local_out = weight_out[0]
    chosen = picks[0, 0].reshape(experts * per_owner)
    send_in = jnp.take(patches[0, 0], chosen, axis=0).reshape(experts, per_owner, dim_model)
    send_grad = jnp.take(grad_out[0, 0], chosen, axis=0).reshape(experts, per_owner, dim_model)
    arrived_in, arrived_grad = exchange(1, send_in, send_grad)
    arrived_in = arrived_in.reshape(owners * per_owner, dim_model)
    arrived_grad = arrived_grad.reshape(owners * per_owner, dim_model)
    group_index = lax.axis_index("dp")
    my_counts = lax.dynamic_index_in_dim(counts[:, :, 0], group_index, 0, keepdims=False)
    my_begins = jnp.cumsum(my_counts) - my_counts
    rank_ids = jnp.arange(per_owner, dtype=jnp.int32)
    slot_of = (my_begins[:, None] + rank_ids[None, :]).reshape(owners * per_owner)
    is_valid = (rank_ids[None, :] < my_counts[:, None]).reshape(owners * per_owner)
    slot_hits = (slot_of[:, None] == jnp.arange(capacity, dtype=jnp.int32)[None, :]) & is_valid[
        :, None
    ]
    slot_hits = slot_hits.astype(jnp.bfloat16)
    rows_in = lax.dot_general(
        slot_hits, arrived_in, (((0,), (0,)), ((), ())), preferred_element_type=jnp.float32
    ).astype(jnp.bfloat16)
    rows_grad = lax.dot_general(
        slot_hits, arrived_grad, (((0,), (0,)), ((), ())), preferred_element_type=jnp.float32
    )
    scaled_rows = (gates[0, 0][:, None] * rows_grad).astype(jnp.bfloat16)
    piece_in, piece_grad = spread(2, rows_in, scaled_rows)
    piece_in = piece_in.reshape(groups * capacity, dim_model)
    piece_grad = piece_grad.reshape(groups * capacity, dim_model)
    preact = jnp.dot(piece_in, local_in, preferred_element_type=jnp.float32)
    gelu_value, gelu_slope = gelu_parts(preact)
    hidden = gelu_value.astype(jnp.bfloat16)
    grad_hidden = lax.dot_general(
        piece_grad, local_out, (((1,), (1,)), ((), ())), preferred_element_type=jnp.float32
    )
    grad_pre = (grad_hidden * gelu_slope).astype(jnp.bfloat16)
    partial = lax.dot_general(
        grad_pre, local_in, (((1,), (1,)), ((), ())), preferred_element_type=jnp.float32
    ).astype(jnp.bfloat16)
    expert_grad = collect(3, partial.reshape(SIDE, SIDE, capacity, dim_model))
    sum_out = lax.dot_general(
        hidden, piece_grad, (((0,), (0,)), ((), ())), preferred_element_type=jnp.float32
    )
    sum_in = lax.dot_general(
        piece_in, grad_pre, (((0,), (0,)), ((), ())), preferred_element_type=jnp.float32
    )
    returned = jnp.dot(slot_hits, expert_grad, preferred_element_type=jnp.float32).astype(
        jnp.bfloat16
    )
    (arrived_back,) = exchange(4, returned.reshape(owners, per_owner, dim_model))
    arrived_back = arrived_back.reshape(experts * per_owner, dim_model)
    owner_table = (jnp.arange(tok_local, dtype=jnp.int32)[:, None] == chosen[None, :]).astype(
        jnp.bfloat16
    )
    grad_local = jnp.dot(owner_table, arrived_back, preferred_element_type=jnp.float32).astype(
        jnp.bfloat16
    )
    return (
        grad_local[None, None],
        sum_in.astype(jnp.bfloat16)[None],
        sum_out.astype(jnp.bfloat16)[None],
    )


def solution(mesh):
    return jax.shard_map(
        on_device,
        mesh=mesh,
        in_specs=(
            P("dp", "expert", None, None),
            P("dp", "expert", None, None),
            P("expert", None, "dp"),
            P("expert", "dp", None),
            P("expert", "dp", None),
            P(None, None, "expert"),
            P("dp", "expert", None, None),
        ),
        out_specs=(P("dp", "expert", None, None), P("expert", None, "dp"), P("expert", "dp", None)),
        check_vma=False,
    )
```

```python
import jax
import jax.numpy as jnp
from jax import lax
from jax.experimental import pallas as pl
from jax.experimental.pallas import tpu as pltpu
from jax.sharding import PartitionSpec as P

MESH = pl.DeviceIdType.MESH
SIDE = 4
HALF = 16
SPLIT = 896
BF16 = jnp.bfloat16
F32 = jnp.float32

gelu_scale = 0.7978845608028654
gelu_cubic = 0.044715


def gelu_parts(preact):
    inner_arg = gelu_scale * (preact + gelu_cubic * preact * preact * preact)
    tangent = jnp.tanh(inner_arg)
    gelu_value = 0.5 * preact * (1.0 + tangent)
    gelu_slope = 0.5 * (1.0 + tangent) + 0.5 * preact * (1.0 - tangent * tangent) * gelu_scale * (
        1.0 + 3.0 * gelu_cubic * preact * preact
    )
    return (gelu_value, gelu_slope)


def wrap(value):
    return lax.rem(value + 2 * SIDE, SIDE)


def place(half, first, second):
    return first * SIDE + second if half == 0 else second * SIDE + first


def one_hot(left, right):
    return (left == right).astype(BF16)


def layer_kernel(
    patches_hbm,
    grad_hbm,
    win_hbm,
    wout_hbm,
    gates,
    pick_col,
    pick_row,
    slot_col,
    slot_row,
    out_patches,
    out_win,
    out_wout,
    patches,
    grads,
    w_in,
    w_out,
    send,
    recv,
    mine,
    full,
    hidden,
    slope,
    grad_pre,
    parts,
    near,
    passing,
    summed,
    last,
    load_sem,
    own_sem,
    cross_send,
    cross_recv,
    spread_send,
    spread_recv,
    sum_send,
    sum_recv,
):
    experts = send.shape[1]
    width = patches.shape[1]
    me = lax.axis_index("expert")
    group = lax.axis_index("dp")
    spot_x, spot_y = lax.div(group, SIDE), lax.rem(group, SIDE)
    barrier = pltpu.get_barrier_semaphore()

    def offset_of(step):
        sign = 1 - 2 * lax.rem(step, 2)
        return experts // 2 + sign * lax.div(step + 1, 2)

    def greet(step, carry):
        peer = lax.rem(me + offset_of(step), experts)
        pl.semaphore_signal(barrier, inc=1, device_id={"expert": peer}, device_id_type=MESH)
        return carry

    lax.fori_loop(0, experts - 1, greet, 0)
    for shift in (1, -1, 2):
        for half in range(2):
            first, second = (spot_x, spot_y) if half == 0 else (spot_y, spot_x)
            pl.semaphore_signal(
                barrier,
                inc=1,
                device_id={"dp": place(half, wrap(first + shift), second)},
                device_id_type=MESH,
            )

    loads = [
        pltpu.make_async_copy(source, target, load_sem.at[i])
        for i, (source, target) in enumerate(
            ((patches_hbm, patches), (grad_hbm, grads), (win_hbm, w_in), (wout_hbm, w_out))
        )
    ]
    for load in loads:
        load.start()

    def cross(i, step, incoming):
        offset = offset_of(step)
        peer = lax.rem(me + (experts - offset if incoming else offset), experts)
        return pltpu.make_async_remote_copy(
            src_ref=send.at[i, peer],
            dst_ref=recv.at[i, peer if incoming else me],
            send_sem=cross_send.at[i, offset],
            recv_sem=cross_recv.at[i, offset],
            device_id={"expert": peer},
            device_id_type=MESH,
        )

    def own_block(i):
        return pltpu.make_async_copy(send.at[i, me], recv.at[i, me], own_sem.at[i])

    def cross_start(i):
        def launch(step, carry):
            cross(i, step, False).start()
            return carry

        lax.fori_loop(0, experts - 1, launch, 0)
        own_block(i).start()

    def cross_wait(i):
        def finish(step, carry):
            cross(i, step, True).wait_recv()
            return carry

        lax.fori_loop(0, experts - 1, finish, 0)
        own_block(i).wait()

    def cross_sent(i):
        def finish(step, carry):
            cross(i, step, False).wait_send()
            return carry

        lax.fori_loop(0, experts - 1, finish, 0)

    pick_hits = one_hot(
        pick_col[...], lax.broadcasted_iota(jnp.int32, (pick_col.shape[0], patches.shape[0]), 1)
    )
    for i, rows in ((0, patches), (1, grads)):
        loads[i].wait()
        chosen = jnp.dot(pick_hits, rows[...], preferred_element_type=F32).astype(BF16)
        send[i] = chosen.reshape(send.shape[1:])
    pl.semaphore_wait(barrier, experts - 1 + 6)
    cross_start(0)
    cross_start(1)

    slot_hits = one_hot(
        lax.broadcasted_iota(jnp.int32, (mine.shape[1], slot_row.shape[1]), 0), slot_row[...]
    )

    def compact(i):
        rows = recv[i].reshape(slot_row.shape[1], width)
        return jnp.dot(slot_hits, rows, preferred_element_type=F32)

    def piece(which, half, stage, move, incoming):
        way = (1, -1, 1, -1)[move]
        first, second = (spot_x, spot_y) if half == 0 else (spot_y, spot_x)
        rows = pl.ds(half * HALF, HALF)
        columns = (
            pl.ds(0, width),
            pl.ds(0, width),
            pl.ds(0, SPLIT),
            pl.ds(SPLIT, width - SPLIT),
        )[move]
        back = (0 if move < 2 else -way) - (way if incoming else 0)
        if stage == 0:
            block = place(half, wrap(first + back), second)
            peer = place(half, wrap(first + way), second)
        else:
            held = wrap(first + (0, -1, 1, 2)[stage - 1])
            block = place(half, held, wrap(second + back))
            peer = place(half, first, wrap(second + way))
        target = full.at[which, block, rows, columns]
        source = target
        if not incoming and move < 2 and stage < 2:
            source = mine.at[which, rows, columns]
        return pltpu.make_async_remote_copy(
            src_ref=source,
            dst_ref=target,
            send_sem=spread_send.at[which, half, stage, move],
            recv_sem=spread_recv.at[which, half, stage, move],
            device_id={"dp": peer},
            device_id_type=MESH,
        )

    def launch(which, half, stage, *moves):
        for move in moves:
            piece(which, half, stage, move, False).start()

    def arrive(which, half, stage, move):
        piece(which, half, stage, move, True).wait_recv()

    def relay(which, half, stage):
        arrive(which, half, stage, 0)
        launch(which, half, stage, 2)
        arrive(which, half, stage, 1)
        launch(which, half, stage, 3)

    def own_rows(which):
        return pltpu.make_async_copy(mine.at[which], full.at[which, group], own_sem.at[3 + which])

    halves = range(2)

    def spread_one(which):
        for stage in (0, 1):
            for half in halves:
                launch(which, half, stage, 0, 1)
        own_rows(which).start()

    def spread_two(which):
        for half in halves:
            arrive(which, half, 0, 0)
            launch(which, half, 0, 2)
            launch(which, half, 2, 0, 1)
            arrive(which, half, 0, 1)
            launch(which, half, 0, 3)
            launch(which, half, 3, 0, 1)

    def spread_three(which):
        for half in halves:
            relay(which, half, 1)
        for half in halves:
            arrive(which, half, 0, 2)
            arrive(which, half, 0, 3)
            launch(which, half, 4, 0, 1)

    def spread_four(which):
        for stage in (2, 3, 4):
            for half in halves:
                relay(which, half, stage)

    def spread_five(which):
        for stage in (1, 2, 3, 4):
            for half in halves:
                arrive(which, half, stage, 2)
                arrive(which, half, stage, 3)
        own_rows(which).wait()

    def spread_sent(which):
        for stage in range(5):
            for half in halves:
                for move in range(4):
                    piece(which, half, stage, move, False).wait_send()

    def stacked(which, chunk):
        rows = full[which, pl.ds(SIDE * chunk, SIDE)]
        return rows.reshape(SIDE * rows.shape[1], width)

    def forward(chunk):
        preact = jnp.dot(stacked(0, chunk), w_in[...], preferred_element_type=F32)
        gelu_value, gelu_slope = gelu_parts(preact)
        hidden[chunk] = gelu_value.astype(BF16)
        slope[chunk] = gelu_slope

    def backward(chunk):
        grad_hidden = lax.dot_general(
            stacked(1, chunk), w_out[...], (((1,), (1,)), ((), ())), preferred_element_type=F32
        )
        value = (grad_hidden * slope[chunk]).astype(BF16)
        grad_pre[chunk] = value
        partial = lax.dot_general(
            value, w_in[...], (((1,), (1,)), ((), ())), preferred_element_type=F32
        )
        parts[chunk] = partial.astype(BF16).reshape(parts.shape[1:])

    cross_wait(0)
    mine[0] = compact(0).astype(BF16)
    spread_one(0)
    spread_two(0)
    spread_three(0)
    spread_four(0)
    spread_five(0)
    loads[2].wait()
    forward(0)
    forward(1)
    cross_wait(1)
    mine[1] = (gates[...] * compact(1)).astype(BF16)
    spread_one(1)
    forward(2)
    spread_two(1)
    forward(3)
    spread_three(1)
    spread_four(1)
    spread_five(1)
    loads[3].wait()

    def unit(half, spot, begin=0, count=SIDE):
        rows = pl.ds(half * HALF, HALF)
        if half == 0:
            return parts.at[spot, pl.ds(begin, count), rows, :]
        return parts.at[pl.ds(begin, count), spot, rows, :]

    def gather_sum(half, move):
        first, second = (spot_x, spot_y) if half == 0 else (spot_y, spot_x)
        if move == 0:
            way, source, target = 1, unit(half, wrap(first + 1)), near.at[half, 0]
        elif move == 1:
            way, source, target = -1, unit(half, wrap(first - 1)), near.at[half, 1]
        elif move == 2:
            way, source, target = 1, unit(half, wrap(first + 2), 0, 2), passing.at[half, 0]
        elif move == 3:
            way, source, target = -1, unit(half, wrap(first + 2), 2, 2), passing.at[half, 1]
        elif move == 4:
            way, source, target = 1, passing.at[half, 0], near.at[half, 2, pl.ds(0, 2)]
        elif move == 5:
            way, source, target = -1, passing.at[half, 1], near.at[half, 2, pl.ds(2, 2)]
        else:
            way = (1, -1, 2)[move - 6]
            source, target = summed.at[half, wrap(second + way)], last.at[half, move - 6]
        if move < 6:
            peer = place(half, wrap(first + way), second)
        else:
            peer = place(half, first, wrap(second + way))
        return pltpu.make_async_remote_copy(
            src_ref=source,
            dst_ref=target,
            send_sem=sum_send.at[half, move],
            recv_sem=sum_recv.at[half, move],
            device_id={"dp": peer},
            device_id_type=MESH,
        )

    backward(wrap(spot_x + 2))
    gather_sum(0, 2).start()
    gather_sum(0, 3).start()
    backward(wrap(spot_x + 1))
    gather_sum(0, 0).start()
    backward(wrap(spot_x - 1))
    gather_sum(0, 1).start()
    backward(spot_x)
    for move in (2, 3, 0, 1):
        gather_sum(1, move).start()
    hidden_rows = hidden[...].reshape(hidden.shape[0] * hidden.shape[1], hidden.shape[2])
    grad_rows = grad_pre[...].reshape(hidden_rows.shape)

    def weight_out(begin, count):
        rows = full[1, :, :, begin : begin + count].reshape(hidden_rows.shape[0], count)
        out_wout[:, begin : begin + count] = lax.dot_general(
            hidden_rows, rows, (((0,), (0,)), ((), ())), preferred_element_type=F32
        ).astype(BF16)

    def weight_in(begin, count):
        rows = full[0, :, :, begin : begin + count].reshape(hidden_rows.shape[0], count)
        out_win[begin : begin + count, :] = lax.dot_general(
            rows, grad_rows, (((0,), (0,)), ((), ())), preferred_element_type=F32
        ).astype(BF16)

    for half in halves:
        gather_sum(half, 2).wait_recv()
        gather_sum(half, 4).start()
        gather_sum(half, 3).wait_recv()
        gather_sum(half, 5).start()
    weight_out(0, width)
    for half in halves:
        for move in (0, 1, 4, 5):
            gather_sum(half, move).wait_recv()
        index = spot_x if half == 0 else spot_y
        for spot in range(SIDE):
            rows = slice(half * HALF, half * HALF + HALF)
            own = parts[index, spot, rows, :] if half == 0 else parts[spot, index, rows, :]
            value = own.astype(F32)
            for source in range(3):
                value = value + near[half, source, spot].astype(F32)
            summed[half, spot] = value.astype(BF16)
        for move in (8, 6, 7):
            gather_sum(half, move).start()
    totals = []
    for half in halves:
        for move in (6, 7, 8):
            gather_sum(half, move).wait_recv()
        index = spot_y if half == 0 else spot_x
        value = summed[half, index].astype(F32)
        for source in range(3):
            value = value + last[half, source].astype(F32)
        totals.append(value.astype(BF16))
    total = jnp.concatenate(totals, axis=0)
    give_hits = one_hot(
        slot_col[...], lax.broadcasted_iota(jnp.int32, (slot_col.shape[0], total.shape[0]), 1)
    )
    returned = jnp.dot(give_hits, total, preferred_element_type=F32).astype(BF16)
    send[2] = returned.reshape(send.shape[1:])
    cross_start(2)
    weight_in(0, SPLIT)
    weight_in(SPLIT, width - SPLIT)
    spread_sent(0)
    spread_sent(1)
    for half in halves:
        for move in range(9):
            gather_sum(half, move).wait_send()
    cross_sent(0)
    cross_sent(1)
    cross_wait(2)
    owner_hits = one_hot(
        lax.broadcasted_iota(jnp.int32, (out_patches.shape[0], pick_row.shape[1]), 0),
        pick_row[...],
    )
    back = recv[2].reshape(pick_row.shape[1], width)
    out_patches[...] = jnp.dot(owner_hits, back, preferred_element_type=F32).astype(BF16)
    cross_sent(2)


def on_device(patches, grad_out, weight_in, weight_out, gates, counts, picks):
    tok_local = patches.shape[2]
    width = patches.shape[3]
    experts = picks.shape[2]
    per_owner = picks.shape[3]
    groups = counts.shape[0]
    owners = counts.shape[1]
    capacity = gates.shape[2]
    units = weight_in.shape[2]
    chosen = picks[0, 0].reshape(experts * per_owner)
    group_index = lax.axis_index("dp")
    my_counts = lax.dynamic_index_in_dim(counts[:, :, 0], group_index, 0, keepdims=False)
    my_begins = jnp.cumsum(my_counts) - my_counts
    rank_ids = jnp.arange(per_owner, dtype=jnp.int32)
    is_valid = rank_ids[None, :] < my_counts[:, None]
    slot_of = jnp.where(is_valid, my_begins[:, None] + rank_ids[None, :], -1)
    slot_of = slot_of.reshape(owners * per_owner)
    in_vmem = pl.BlockSpec(memory_space=pltpu.VMEM)
    in_place = pl.BlockSpec(memory_space=pl.ANY)
    rows = groups * capacity
    side_rows = rows // SIDE
    slab = (experts, per_owner, width)
    grad_patches, grad_in, grad_out_weight = pl.pallas_call(
        layer_kernel,
        out_shape=[
            jax.ShapeDtypeStruct((tok_local, width), BF16),
            jax.ShapeDtypeStruct((width, units), BF16),
            jax.ShapeDtypeStruct((units, width), BF16),
        ],
        in_specs=[in_place] * 4 + [in_vmem] * 5,
        out_specs=[in_vmem] * 3,
        scratch_shapes=[
            pltpu.VMEM((tok_local, width), BF16),
            pltpu.VMEM((tok_local, width), BF16),
            pltpu.VMEM((width, units), BF16),
            pltpu.VMEM((units, width), BF16),
            pltpu.VMEM((3,) + slab, BF16),
            pltpu.VMEM((3,) + slab, BF16),
            pltpu.VMEM((2, capacity, width), BF16),
            pltpu.VMEM((2, groups, capacity, width), BF16),
            pltpu.VMEM((SIDE, side_rows, units), BF16),
            pltpu.VMEM((SIDE, side_rows, units), F32),
            pltpu.VMEM((SIDE, side_rows, units), BF16),
            pltpu.VMEM((SIDE, SIDE, capacity, width), BF16),
            pltpu.VMEM((2, 3, SIDE, HALF, width), BF16),
            pltpu.VMEM((2, 2, 2, HALF, width), BF16),
            pltpu.VMEM((2, SIDE, HALF, width), BF16),
            pltpu.VMEM((2, 3, HALF, width), BF16),
            pltpu.SemaphoreType.DMA((4,)),
            pltpu.SemaphoreType.DMA((5,)),
            pltpu.SemaphoreType.DMA((3, experts)),
            pltpu.SemaphoreType.DMA((3, experts)),
            pltpu.SemaphoreType.DMA((2, 2, 5, 4)),
            pltpu.SemaphoreType.DMA((2, 2, 5, 4)),
            pltpu.SemaphoreType.DMA((2, 9)),
            pltpu.SemaphoreType.DMA((2, 9)),
        ],
        compiler_params=pltpu.CompilerParams(
            collective_id=1, has_side_effects=True, vmem_limit_bytes=56 * 1024 * 1024
        ),
    )(
        patches[0, 0],
        grad_out[0, 0],
        weight_in[0],
        weight_out[0],
        gates[0, 0][:, None],
        chosen[:, None],
        chosen[None, :],
        slot_of[:, None],
        slot_of[None, :],
    )
    return (grad_patches[None, None], grad_in[None], grad_out_weight[None])


def solution(mesh):
    return jax.shard_map(
        on_device,
        mesh=mesh,
        in_specs=(
            P("dp", "expert", None, None),
            P("dp", "expert", None, None),
            P("expert", None, "dp"),
            P("expert", "dp", None),
            P("expert", "dp", None),
            P(None, None, "expert"),
            P("dp", "expert", None, None),
        ),
        out_specs=(P("dp", "expert", None, None), P("expert", None, "dp"), P("expert", "dp", None)),
        check_vma=False,
    )
```

```python
import jax
import jax.numpy as jnp
from jax import lax
from jax.experimental import pallas as pl
from jax.experimental.pallas import tpu as pltpu
from jax.sharding import PartitionSpec as P

MESH = pl.DeviceIdType.MESH
SIDE = 4
HALF = 16
CUT = 896
BF16 = jnp.bfloat16
F32 = jnp.float32

gelu_scale = 0.7978845608028654
gelu_cubic = 0.044715


def gelu_parts(preact):
    inner_arg = gelu_scale * (preact + gelu_cubic * preact * preact * preact)
    tangent = jnp.tanh(inner_arg)
    gelu_value = 0.5 * preact * (1.0 + tangent)
    gelu_slope = 0.5 * (1.0 + tangent) + 0.5 * preact * (1.0 - tangent * tangent) * gelu_scale * (
        1.0 + 3.0 * gelu_cubic * preact * preact
    )
    return (gelu_value, gelu_slope)


def wrap(value):
    return lax.rem(value + 2 * SIDE, SIDE)


def place(half, first, second):
    return first * SIDE + second if half == 0 else second * SIDE + first


def widths_of(width):
    return ((0, width), (0, CUT), (CUT, width - CUT))


def pick_table(picks, tokens):
    ranks, experts = picks.shape
    total = ranks * experts
    owner = lax.broadcasted_iota(jnp.int32, (experts, total), 0)
    entry = lax.broadcasted_iota(jnp.int32, (experts, total), 1)
    row = jnp.zeros((1, total), F32)
    for rank in range(ranks):
        spread_out = (entry == ranks * owner + rank).astype(BF16)
        values = picks[rank : rank + 1, :].astype(F32).astype(BF16)
        row = row + jnp.dot(values, spread_out, preferred_element_type=F32)
    token = lax.broadcasted_iota(jnp.int32, (tokens, total), 0)
    return (token == row.astype(jnp.int32)).astype(BF16)


def slot_table(counts, capacity, ranks):
    owners = counts.shape[1]
    total = ranks * owners
    owner = lax.broadcasted_iota(jnp.int32, (owners, total), 0)
    entry = lax.broadcasted_iota(jnp.int32, (owners, total), 1)
    before = (ranks * owner + ranks <= entry).astype(BF16)
    here = ((ranks * owner <= entry) & (entry < ranks * owner + ranks)).astype(BF16)
    taken = counts.astype(F32).astype(BF16)
    begin = jnp.dot(taken, before, preferred_element_type=F32)
    count = jnp.dot(taken, here, preferred_element_type=F32)
    rank = lax.rem(lax.broadcasted_iota(jnp.int32, (1, total), 1), ranks).astype(F32)
    slot = jnp.where(rank < count, begin + rank, -1.0).astype(jnp.int32)
    row = lax.broadcasted_iota(jnp.int32, (capacity, total), 0)
    return (row == slot).astype(BF16)


def layer_kernel(*refs):
    (patches_hbm, grad_hbm, win_hbm, wout_hbm, gates, counts, picks) = refs[:7]
    back = refs[7:9]
    out_win, out_wout = refs[9:11]
    (patches, grads, w_in, w_out, hold_win, hold_wout) = refs[11:17]
    send = refs[17:22]
    recv = refs[22:25] + back
    mine = refs[25:28]
    full = refs[28:31]
    (hidden, slope, early, grad_pre) = refs[31:35]
    parts = refs[35:37]
    near = refs[37:39]
    passing = refs[39:41]
    summed = refs[41:43]
    last = refs[43:45]
    (load_sem, own_sem, cross_send, cross_recv) = refs[45:49]
    (spread_send, spread_recv, sum_send, sum_recv) = refs[49:]
    experts, ranks = send[0].shape[:2]
    capacity = mine[0].shape[0]
    width = patches.shape[1]
    spans = widths_of(width)
    me = lax.axis_index("expert")
    group = lax.axis_index("dp")
    spot_x, spot_y = lax.div(group, SIDE), lax.rem(group, SIDE)
    barrier = pltpu.get_barrier_semaphore()

    def offset_of(step):
        sign = 1 - 2 * lax.rem(step, 2)
        return experts // 2 + sign * lax.div(step + 1, 2)

    def greet(step, carry):
        peer = lax.rem(me + offset_of(step), experts)
        pl.semaphore_signal(barrier, inc=1, device_id={"expert": peer}, device_id_type=MESH)
        return carry

    lax.fori_loop(0, experts - 1, greet, 0)
    for shift in (1, -1, 2):
        for half in range(2):
            first, second = (spot_x, spot_y) if half == 0 else (spot_y, spot_x)
            pl.semaphore_signal(
                barrier,
                inc=1,
                device_id={"dp": place(half, wrap(first + shift), second)},
                device_id_type=MESH,
            )

    loads = [
        pltpu.make_async_copy(source, target, load_sem.at[i])
        for i, (source, target) in enumerate(
            ((patches_hbm, patches), (grad_hbm, grads), (win_hbm, w_in), (wout_hbm, w_out))
        )
    ]
    for load in loads:
        load.start()

    def cross(i, step, incoming):
        offset = offset_of(step)
        peer = lax.rem(me + (experts - offset if incoming else offset), experts)
        return pltpu.make_async_remote_copy(
            src_ref=send[i].at[peer],
            dst_ref=recv[i].at[peer if incoming else me],
            send_sem=cross_send.at[i, offset],
            recv_sem=cross_recv.at[i, offset],
            device_id={"expert": peer},
            device_id_type=MESH,
        )

    def own_block(i):
        return pltpu.make_async_copy(send[i].at[me], recv[i].at[me], own_sem.at[i])

    def cross_start(i):
        def launch(step, carry):
            cross(i, step, False).start()
            return carry

        lax.fori_loop(0, experts - 1, launch, 0)
        own_block(i).start()

    def cross_wait(i):
        def finish(step, carry):
            cross(i, step, True).wait_recv()
            return carry

        lax.fori_loop(0, experts - 1, finish, 0)
        own_block(i).wait()

    def cross_sent(i):
        def finish(step, carry):
            cross(i, step, False).wait_send()
            return carry

        lax.fori_loop(0, experts - 1, finish, 0)

    pick_hits = pick_table(picks, patches.shape[0])
    slot_hits = slot_table(counts[group], capacity, ranks)
    diagonal = lax.broadcasted_iota(jnp.int32, (capacity, capacity), 0) == (
        lax.broadcasted_iota(jnp.int32, (capacity, capacity), 1)
    )
    gate_col = jnp.sum(jnp.where(diagonal, gates[...], 0.0), axis=1, keepdims=True)

    def turned(left, right):
        return lax.dot_general(left, right, (((0,), (0,)), ((), ())), preferred_element_type=F32)

    loads[0].wait()
    send[0][...] = turned(pick_hits, patches[...]).astype(BF16).reshape(send[0].shape)
    loads[1].wait()
    chosen = turned(pick_hits, grads[...]).astype(BF16)
    for i in (1, 2):
        begin, count = spans[i]
        send[i][...] = chosen[:, begin : begin + count].reshape(send[i].shape)
    pl.semaphore_wait(barrier, experts - 1 + 6)
    for i in range(3):
        cross_start(i)

    def compact(i):
        rows = recv[i][...].reshape(ranks * experts, spans[i][1])
        return jnp.dot(slot_hits, rows, preferred_element_type=F32)

    def piece(which, half, stage, move, incoming):
        way = (1, -1, 1, -1)[move]
        first, second = (spot_x, spot_y) if half == 0 else (spot_y, spot_x)
        rows = pl.ds(half * HALF, HALF)
        wide = spans[which][1]
        split = (wide // 256 + 1) * 128 if wide % 256 else wide // 2
        columns = (pl.ds(0, wide), pl.ds(0, wide), pl.ds(0, split), pl.ds(split, wide - split))[
            move
        ]
        back_by = (0 if move < 2 else -way) - (way if incoming else 0)
        if stage == 0:
            block = place(half, wrap(first + back_by), second)
            peer = place(half, wrap(first + way), second)
        else:
            held = wrap(first + (0, -1, 1, 2)[stage - 1])
            block = place(half, held, wrap(second + back_by))
            peer = place(half, first, wrap(second + way))
        target = full[which].at[block, rows, columns]
        source = target
        if not incoming and move < 2 and stage < 2:
            source = mine[which].at[rows, columns]
        return pltpu.make_async_remote_copy(
            src_ref=source,
            dst_ref=target,
            send_sem=spread_send.at[which, half, stage, move],
            recv_sem=spread_recv.at[which, half, stage, move],
            device_id={"dp": peer},
            device_id_type=MESH,
        )

    def launch(which, half, stage, *moves):
        for move in moves:
            piece(which, half, stage, move, False).start()

    def arrive(which, half, stage, move):
        piece(which, half, stage, move, True).wait_recv()

    def relay(which, half, stage):
        arrive(which, half, stage, 0)
        launch(which, half, stage, 2)
        arrive(which, half, stage, 1)
        launch(which, half, stage, 3)

    def own_rows(which):
        return pltpu.make_async_copy(mine[which], full[which].at[group], own_sem.at[5 + which])

    halves = range(2)

    def spread_one(which):
        for stage in (0, 1):
            for half in halves:
                launch(which, half, stage, 0, 1)
        own_rows(which).start()

    def spread_two(which):
        for half in halves:
            arrive(which, half, 0, 0)
            launch(which, half, 0, 2)
            launch(which, half, 2, 0, 1)
            arrive(which, half, 0, 1)
            launch(which, half, 0, 3)
            launch(which, half, 3, 0, 1)

    def spread_three(which):
        for half in halves:
            relay(which, half, 1)
        for half in halves:
            arrive(which, half, 0, 2)
            arrive(which, half, 0, 3)
            launch(which, half, 4, 0, 1)

    def spread_four(which):
        for stage in (2, 3, 4):
            for half in halves:
                relay(which, half, stage)

    def spread_five(which):
        for stage in (1, 2, 3, 4):
            for half in halves:
                arrive(which, half, stage, 2)
                arrive(which, half, stage, 3)
        own_rows(which).wait()

    def spread_sent(which):
        for stage in range(5):
            for half in halves:
                for move in range(4):
                    piece(which, half, stage, move, False).wait_send()

    def stacked(which, chunk):
        rows = full[which][pl.ds(SIDE * chunk, SIDE)]
        return rows.reshape(SIDE * capacity, spans[which][1])

    def forward(chunk):
        preact = jnp.dot(stacked(0, chunk), w_in[...], preferred_element_type=F32)
        gelu_value, gelu_slope = gelu_parts(preact)
        hidden[chunk] = gelu_value.astype(BF16)
        slope[chunk] = gelu_slope

    def pull(which, chunk):
        begin, count = spans[which]
        return lax.dot_general(
            stacked(which, chunk),
            w_out[:, begin : begin + count],
            (((1,), (1,)), ((), ())),
            preferred_element_type=F32,
        )

    def backward(chunk):
        grad_hidden = early[chunk] + pull(2, chunk)
        grad_pre[chunk] = (grad_hidden * slope[chunk]).astype(BF16)

    def project(part, chunk):
        begin, count = spans[1 + part]
        partial = lax.dot_general(
            grad_pre[chunk],
            w_in[begin : begin + count, :],
            (((1,), (1,)), ((), ())),
            preferred_element_type=F32,
        )
        parts[part][chunk] = partial.astype(BF16).reshape(parts[part].shape[1:])

    cross_wait(0)
    mine[0][...] = compact(0).astype(BF16)
    spread_one(0)
    spread_two(0)
    spread_three(0)
    spread_four(0)
    spread_five(0)
    cross_wait(1)
    mine[1][...] = (gate_col * compact(1)).astype(BF16)
    spread_one(1)
    loads[2].wait()
    forward(0)
    spread_two(1)
    forward(1)
    spread_three(1)
    spread_four(1)
    spread_five(1)
    cross_wait(2)
    mine[2][...] = (gate_col * compact(2)).astype(BF16)
    spread_one(2)
    forward(2)
    spread_two(2)
    forward(3)
    spread_three(2)
    loads[3].wait()
    for chunk in range(SIDE):
        early[chunk] = pull(1, chunk)
    spread_four(2)
    spread_five(2)

    def unit(part, half, spot, begin=0, count=SIDE):
        rows = pl.ds(half * HALF, HALF)
        if half == 0:
            return parts[part].at[spot, pl.ds(begin, count), rows, :]
        return parts[part].at[pl.ds(begin, count), spot, rows, :]

    def tally(part, half, move):
        first, second = (spot_x, spot_y) if half == 0 else (spot_y, spot_x)
        close, through = near[part], passing[part]
        if move == 0:
            way, source, target = 1, unit(part, half, wrap(first + 1)), close.at[half, 0]
        elif move == 1:
            way, source, target = -1, unit(part, half, wrap(first - 1)), close.at[half, 1]
        elif move == 2:
            way, source, target = 1, unit(part, half, wrap(first + 2), 0, 2), through.at[half, 0]
        elif move == 3:
            way, source, target = -1, unit(part, half, wrap(first + 2), 2, 2), through.at[half, 1]
        elif move == 4:
            way, source, target = 1, through.at[half, 0], close.at[half, 2, pl.ds(0, 2)]
        elif move == 5:
            way, source, target = -1, through.at[half, 1], close.at[half, 2, pl.ds(2, 2)]
        else:
            way = (1, -1, 2)[move - 6]
            source = summed[part].at[half, wrap(second + way)]
            target = last[part].at[half, move - 6]
        if move < 6:
            peer = place(half, wrap(first + way), second)
        else:
            peer = place(half, first, wrap(second + way))
        return pltpu.make_async_remote_copy(
            src_ref=source,
            dst_ref=target,
            send_sem=sum_send.at[part, half, move],
            recv_sem=sum_recv.at[part, half, move],
            device_id={"dp": peer},
            device_id_type=MESH,
        )

    def tally_relay(part):
        for half in halves:
            tally(part, half, 2).wait_recv()
            tally(part, half, 4).start()
            tally(part, half, 3).wait_recv()
            tally(part, half, 5).start()

    def tally_near(part):
        for half in halves:
            for move in (0, 1, 4, 5):
                tally(part, half, move).wait_recv()
            index = spot_x if half == 0 else spot_y
            rows = slice(half * HALF, half * HALF + HALF)
            for spot in range(SIDE):
                if half == 0:
                    own = parts[part][index, spot, rows, :]
                else:
                    own = parts[part][spot, index, rows, :]
                value = own.astype(F32)
                for source in range(3):
                    value = value + near[part][half, source, spot].astype(F32)
                summed[part][half, spot] = value.astype(BF16)
            for move in (8, 6, 7):
                tally(part, half, move).start()

    def give_back(part):
        totals = []
        for half in halves:
            for move in (6, 7, 8):
                tally(part, half, move).wait_recv()
            index = spot_y if half == 0 else spot_x
            value = summed[part][half, index].astype(F32)
            for source in range(3):
                value = value + last[part][half, source].astype(F32)
            totals.append(value.astype(BF16))
        total = jnp.concatenate(totals, axis=0)
        send[3 + part][...] = turned(slot_hits, total).astype(BF16).reshape(send[3 + part].shape)
        cross_start(3 + part)

    backward(wrap(spot_x + 2))
    project(0, wrap(spot_x + 2))
    tally(0, 0, 2).start()
    tally(0, 0, 3).start()
    backward(wrap(spot_x + 1))
    project(0, wrap(spot_x + 1))
    tally(0, 0, 0).start()
    backward(wrap(spot_x - 1))
    project(0, wrap(spot_x - 1))
    tally(0, 0, 1).start()
    backward(spot_x)
    project(0, spot_x)
    for move in (2, 3, 0, 1):
        tally(0, 1, move).start()
    for chunk in range(SIDE):
        project(1, chunk)
    tally_relay(0)
    for move in (2, 3, 0, 1):
        for half in halves:
            tally(1, half, move).start()
    hidden_rows = hidden[...].reshape(SIDE * hidden.shape[1], hidden.shape[2])
    grad_rows = grad_pre[...].reshape(hidden_rows.shape)

    def weight_out(which):
        begin, count = spans[which]
        rows = full[which][...].reshape(hidden_rows.shape[0], count)
        hold_wout[:, begin : begin + count] = turned(hidden_rows, rows).astype(BF16)

    def weight_in(begin, count):
        rows = full[0][:, :, begin : begin + count].reshape(hidden_rows.shape[0], count)
        hold_win[begin : begin + count, :] = turned(rows, grad_rows).astype(BF16)

    weight_out(1)
    tally_near(0)
    tally_relay(1)
    give_back(0)
    tally_near(1)
    weight_out(2)
    give_back(1)
    store_wout = pltpu.make_async_copy(hold_wout, out_wout, load_sem.at[4])
    store_wout.start()
    weight_in(*spans[1])
    weight_in(*spans[2])
    store_win = pltpu.make_async_copy(hold_win, out_win, load_sem.at[5])
    store_win.start()
    for which in range(3):
        spread_sent(which)
    for part in range(2):
        for half in halves:
            for move in range(9):
                tally(part, half, move).wait_send()
    for i in range(3):
        cross_sent(i)
    cross_wait(3)
    cross_wait(4)
    cross_sent(3)
    cross_sent(4)
    store_wout.wait()
    store_win.wait()


def tail_kernel(
    picks, back_a, back_b, win_hbm, wout_hbm, out_patches, out_win, out_wout, win, wout, sem_in, sem_out
):
    width = out_patches.shape[1]
    loads, stores = [], []
    for i, (source, held, target) in enumerate(((win_hbm, win, out_win), (wout_hbm, wout, out_wout))):
        step = source.shape[0] // 2
        for half in range(2):
            rows = pl.ds(half * step, step)
            at = 2 * i + half
            loads.append(pltpu.make_async_copy(source.at[rows], held.at[rows], sem_in.at[at]))
            stores.append(pltpu.make_async_copy(held.at[rows], target.at[rows], sem_out.at[at]))
    for load in loads:
        load.start()
    owner_hits = pick_table(picks, out_patches.shape[0])
    for (begin, count), back in zip(widths_of(width)[1:], (back_a, back_b)):
        rows = back[...].reshape(back.shape[0] * back.shape[1], count)
        out_patches[:, begin : begin + count] = jnp.dot(
            owner_hits, rows, preferred_element_type=F32
        ).astype(BF16)
    for load, store in zip(loads, stores):
        load.wait()
        store.start()
    for store in stores:
        store.wait()


def on_device(patches, grad_out, weight_in, weight_out, gates, counts, picks):
    tokens = patches.shape[2]
    width = patches.shape[3]
    experts = picks.shape[2]
    ranks = picks.shape[3]
    groups = counts.shape[0]
    capacity = gates.shape[2]
    units = weight_in.shape[2]
    side_rows = groups * capacity // SIDE
    parts = [count for _, count in widths_of(width)]
    in_vmem = pl.BlockSpec(memory_space=pltpu.VMEM)
    in_place = pl.BlockSpec(memory_space=pl.ANY)
    shape_in = jax.ShapeDtypeStruct((width, units), BF16)
    shape_out = jax.ShapeDtypeStruct((units, width), BF16)
    local_picks = jnp.transpose(picks[0, 0])
    slabs = [pltpu.VMEM((experts, ranks, count), BF16) for count in parts + parts[1:]]
    back_a, back_b, grad_in, grad_out_weight = pl.pallas_call(
        layer_kernel,
        out_shape=[jax.ShapeDtypeStruct((experts, ranks, count), BF16) for count in parts[1:]]
        + [shape_in, shape_out],
        in_specs=[in_place] * 4 + [in_vmem] * 3,
        out_specs=[in_vmem] * 2 + [in_place] * 2,
        scratch_shapes=[
            pltpu.VMEM((tokens, width), BF16),
            pltpu.VMEM((tokens, width), BF16),
            pltpu.VMEM((width, units), BF16),
            pltpu.VMEM((units, width), BF16),
            pltpu.VMEM((width, units), BF16),
            pltpu.VMEM((units, width), BF16),
        ]
        + slabs
        + slabs[:3]
        + [pltpu.VMEM((capacity, count), BF16) for count in parts]
        + [pltpu.VMEM((groups, capacity, count), BF16) for count in parts]
        + [
            pltpu.VMEM((SIDE, side_rows, units), BF16),
            pltpu.VMEM((SIDE, side_rows, units), F32),
            pltpu.VMEM((SIDE, side_rows, units), F32),
            pltpu.VMEM((SIDE, side_rows, units), BF16),
        ]
        + [pltpu.VMEM((SIDE, SIDE, capacity, count), BF16) for count in parts[1:]]
        + [pltpu.VMEM((2, 3, SIDE, HALF, count), BF16) for count in parts[1:]]
        + [pltpu.VMEM((2, 2, 2, HALF, count), BF16) for count in parts[1:]]
        + [pltpu.VMEM((2, SIDE, HALF, count), BF16) for count in parts[1:]]
        + [pltpu.VMEM((2, 3, HALF, count), BF16) for count in parts[1:]]
        + [
            pltpu.SemaphoreType.DMA((6,)),
            pltpu.SemaphoreType.DMA((8,)),
            pltpu.SemaphoreType.DMA((5, experts)),
            pltpu.SemaphoreType.DMA((5, experts)),
            pltpu.SemaphoreType.DMA((3, 2, 5, 4)),
            pltpu.SemaphoreType.DMA((3, 2, 5, 4)),
            pltpu.SemaphoreType.DMA((2, 2, 9)),
            pltpu.SemaphoreType.DMA((2, 2, 9)),
        ],
        compiler_params=pltpu.CompilerParams(
            collective_id=1, has_side_effects=True, vmem_limit_bytes=56 * 1024 * 1024
        ),
    )(
        patches[0, 0],
        grad_out[0, 0],
        weight_in[0],
        weight_out[0],
        gates[0],
        jnp.transpose(counts, (0, 2, 1)),
        local_picks,
    )
    grad_patches, grad_in, grad_out_weight = pl.pallas_call(
        tail_kernel,
        out_shape=[jax.ShapeDtypeStruct((tokens, width), BF16), shape_in, shape_out],
        in_specs=[in_vmem] * 3 + [in_place] * 2,
        out_specs=[in_vmem] + [in_place] * 2,
        scratch_shapes=[
            pltpu.VMEM((width, units), BF16),
            pltpu.VMEM((units, width), BF16),
            pltpu.SemaphoreType.DMA((4,)),
            pltpu.SemaphoreType.DMA((4,)),
        ],
        compiler_params=pltpu.CompilerParams(vmem_limit_bytes=56 * 1024 * 1024),
    )(local_picks, back_a, back_b, grad_in, grad_out_weight)
    return (grad_patches[None, None], grad_in[None], grad_out_weight[None])


def solution(mesh):
    return jax.shard_map(
        on_device,
        mesh=mesh,
        in_specs=(
            P("dp", "expert", None, None),
            P("dp", "expert", None, None),
            P("expert", None, "dp"),
            P("expert", "dp", None),
            P("expert", "dp", None),
            P(None, None, "expert"),
            P("dp", "expert", None, None),
        ),
        out_specs=(P("dp", "expert", None, None), P("expert", None, "dp"), P("expert", "dp", None)),
        check_vma=False,
    )
```

```python
import jax
import jax.numpy as jnp
from jax import lax
from jax.experimental import pallas as pl
from jax.experimental.pallas import tpu as pltpu
from jax.sharding import PartitionSpec as P

MESH = pl.DeviceIdType.MESH
SIDE = 4
HALF = 16
CUT = 896
BF16 = jnp.bfloat16
F32 = jnp.float32

gelu_scale = 0.7978845608028654
gelu_cubic = 0.044715


def gelu_parts(preact):
    inner_arg = gelu_scale * (preact + gelu_cubic * preact * preact * preact)
    tangent = jnp.tanh(inner_arg)
    gelu_value = 0.5 * preact * (1.0 + tangent)
    gelu_slope = 0.5 * (1.0 + tangent) + 0.5 * preact * (1.0 - tangent * tangent) * gelu_scale * (
        1.0 + 3.0 * gelu_cubic * preact * preact
    )
    return (gelu_value, gelu_slope)


def wrap(value):
    return lax.rem(value + 2 * SIDE, SIDE)


def place(half, first, second):
    return first * SIDE + second if half == 0 else second * SIDE + first


def widths_of(width):
    return ((0, width), (0, width))


def pick_table(picks, tokens):
    ranks, experts = picks.shape
    total = ranks * experts
    owner = lax.broadcasted_iota(jnp.int32, (experts, total), 0)
    entry = lax.broadcasted_iota(jnp.int32, (experts, total), 1)
    row = jnp.zeros((1, total), F32)
    for rank in range(ranks):
        spread_out = (entry == ranks * owner + rank).astype(BF16)
        values = picks[rank : rank + 1, :].astype(F32).astype(BF16)
        row = row + jnp.dot(values, spread_out, preferred_element_type=F32)
    token = lax.broadcasted_iota(jnp.int32, (tokens, total), 0)
    return (token == row.astype(jnp.int32)).astype(BF16)


def slot_table(counts, capacity, ranks):
    owners = counts.shape[1]
    total = ranks * owners
    owner = lax.broadcasted_iota(jnp.int32, (owners, total), 0)
    entry = lax.broadcasted_iota(jnp.int32, (owners, total), 1)
    before = (ranks * owner + ranks <= entry).astype(BF16)
    here = ((ranks * owner <= entry) & (entry < ranks * owner + ranks)).astype(BF16)
    taken = counts.astype(F32).astype(BF16)
    begin = jnp.dot(taken, before, preferred_element_type=F32)
    count = jnp.dot(taken, here, preferred_element_type=F32)
    rank = lax.rem(lax.broadcasted_iota(jnp.int32, (1, total), 1), ranks).astype(F32)
    slot = jnp.where(rank < count, begin + rank, -1.0).astype(jnp.int32)
    row = lax.broadcasted_iota(jnp.int32, (capacity, total), 0)
    return (row == slot).astype(BF16)


def layer_kernel(*refs):
    (patches_hbm, grad_hbm, win_hbm, wout_hbm, gates, counts, picks) = refs[:7]
    back = refs[7:8]
    out_win, out_wout = refs[8:10]
    (patches, grads, w_in, w_out, hold_win, hold_wout) = refs[10:16]
    send = refs[16:19]
    recv = refs[19:21] + back
    mine = refs[21:23]
    full = refs[23:25]
    (hidden, slope, grad_pre, parts, near, passing, summed, last) = refs[25:33]
    (load_sem, own_sem, cross_send, cross_recv) = refs[33:37]
    (spread_send, spread_recv, sum_send, sum_recv) = refs[37:]
    experts, ranks = send[0].shape[:2]
    capacity = mine[0].shape[0]
    width = patches.shape[1]
    spans = widths_of(width)
    me = lax.axis_index("expert")
    group = lax.axis_index("dp")
    spot_x, spot_y = lax.div(group, SIDE), lax.rem(group, SIDE)
    barrier = pltpu.get_barrier_semaphore()

    def offset_of(step):
        sign = 1 - 2 * lax.rem(step, 2)
        return experts // 2 + sign * lax.div(step + 1, 2)

    def greet(step, carry):
        peer = lax.rem(me + offset_of(step), experts)
        pl.semaphore_signal(barrier, inc=1, device_id={"expert": peer}, device_id_type=MESH)
        return carry

    lax.fori_loop(0, experts - 1, greet, 0)
    for shift in (1, -1, 2):
        for half in range(2):
            first, second = (spot_x, spot_y) if half == 0 else (spot_y, spot_x)
            pl.semaphore_signal(
                barrier,
                inc=1,
                device_id={"dp": place(half, wrap(first + shift), second)},
                device_id_type=MESH,
            )

    loads = [
        pltpu.make_async_copy(source, target, load_sem.at[i])
        for i, (source, target) in enumerate(
            ((patches_hbm, patches), (grad_hbm, grads), (win_hbm, w_in), (wout_hbm, w_out))
        )
    ]
    for load in loads:
        load.start()

    def cross(i, step, incoming):
        offset = offset_of(step)
        peer = lax.rem(me + (experts - offset if incoming else offset), experts)
        return pltpu.make_async_remote_copy(
            src_ref=send[i].at[peer],
            dst_ref=recv[i].at[peer if incoming else me],
            send_sem=cross_send.at[i, offset],
            recv_sem=cross_recv.at[i, offset],
            device_id={"expert": peer},
            device_id_type=MESH,
        )

    def own_block(i):
        return pltpu.make_async_copy(send[i].at[me], recv[i].at[me], own_sem.at[i])

    def cross_start(i, begin=0, end=experts - 1):
        def launch(step, carry):
            cross(i, step, False).start()
            return carry

        lax.fori_loop(begin, end, launch, 0)
        if begin == 0:
            own_block(i).start()

    def cross_wait(i):
        def finish(step, carry):
            cross(i, step, True).wait_recv()
            return carry

        lax.fori_loop(0, experts - 1, finish, 0)
        own_block(i).wait()

    def cross_sent(i):
        def finish(step, carry):
            cross(i, step, False).wait_send()
            return carry

        lax.fori_loop(0, experts - 1, finish, 0)

    pick_hits = pick_table(picks, patches.shape[0])
    slot_hits = slot_table(counts[group], capacity, ranks)
    diagonal = lax.broadcasted_iota(jnp.int32, (capacity, capacity), 0) == (
        lax.broadcasted_iota(jnp.int32, (capacity, capacity), 1)
    )
    gate_col = jnp.sum(jnp.where(diagonal, gates[...], 0.0), axis=1, keepdims=True)

    def turned(left, right):
        return lax.dot_general(left, right, (((0,), (0,)), ((), ())), preferred_element_type=F32)

    loads[0].wait()
    send[0][...] = turned(pick_hits, patches[...]).astype(BF16).reshape(send[0].shape)
    loads[1].wait()
    send[1][...] = turned(pick_hits, grads[...]).astype(BF16).reshape(send[1].shape)
    pl.semaphore_wait(barrier, experts - 1 + 6)
    cross_start(0)
    cross_start(1)

    def compact(i):
        rows = recv[i][...].reshape(ranks * experts, spans[i][1])
        return jnp.dot(slot_hits, rows, preferred_element_type=F32)

    def piece(which, half, stage, move, incoming):
        way = (1, -1, 1, -1)[move]
        first, second = (spot_x, spot_y) if half == 0 else (spot_y, spot_x)
        rows = pl.ds(half * HALF, HALF)
        wide = spans[which][1]
        split = (wide // 256 + 1) * 128 if wide % 256 else wide // 2
        columns = (pl.ds(0, wide), pl.ds(0, wide), pl.ds(0, split), pl.ds(split, wide - split))[
            move
        ]
        back_by = (0 if move < 2 else -way) - (way if incoming else 0)
        if stage == 0:
            block = place(half, wrap(first + back_by), second)
            peer = place(half, wrap(first + way), second)
        else:
            held = wrap(first + (0, -1, 1, 2)[stage - 1])
            block = place(half, held, wrap(second + back_by))
            peer = place(half, first, wrap(second + way))
        target = full[which].at[block, rows, columns]
        source = target
        if not incoming and move < 2 and stage < 2:
            source = mine[which].at[rows, columns]
        return pltpu.make_async_remote_copy(
            src_ref=source,
            dst_ref=target,
            send_sem=spread_send.at[which, half, stage, move],
            recv_sem=spread_recv.at[which, half, stage, move],
            device_id={"dp": peer},
            device_id_type=MESH,
        )

    def launch(which, half, stage, *moves):
        for move in moves:
            piece(which, half, stage, move, False).start()

    def arrive(which, half, stage, move):
        piece(which, half, stage, move, True).wait_recv()

    def relay(which, half, stage):
        arrive(which, half, stage, 0)
        launch(which, half, stage, 2)
        arrive(which, half, stage, 1)
        launch(which, half, stage, 3)

    def own_rows(which):
        return pltpu.make_async_copy(mine[which], full[which].at[group], own_sem.at[3 + which])

    halves = range(2)

    def spread_one(which):
        for stage in (0, 1):
            for half in halves:
                launch(which, half, stage, 0, 1)
        own_rows(which).start()

    def spread_two(which):
        for half in halves:
            arrive(which, half, 0, 0)
            launch(which, half, 0, 2)
            launch(which, half, 2, 0, 1)
            arrive(which, half, 0, 1)
            launch(which, half, 0, 3)
            launch(which, half, 3, 0, 1)

    def spread_three(which):
        for half in halves:
            relay(which, half, 1)
        for half in halves:
            arrive(which, half, 0, 2)
            arrive(which, half, 0, 3)
            launch(which, half, 4, 0, 1)

    def spread_four(which):
        for stage in (2, 3, 4):
            for half in halves:
                relay(which, half, stage)

    def spread_five(which):
        for stage in (1, 2, 3, 4):
            for half in halves:
                arrive(which, half, stage, 2)
                arrive(which, half, stage, 3)
        own_rows(which).wait()

    def spread_sent(which):
        for stage in range(5):
            for half in halves:
                for move in range(4):
                    piece(which, half, stage, move, False).wait_send()

    def stacked(which, chunk):
        rows = full[which][pl.ds(SIDE * chunk, SIDE)]
        return rows.reshape(SIDE * capacity, spans[which][1])

    def forward(chunk):
        preact = jnp.dot(stacked(0, chunk), w_in[...], preferred_element_type=F32)
        gelu_value, gelu_slope = gelu_parts(preact)
        hidden[chunk] = gelu_value.astype(BF16)
        slope[chunk] = gelu_slope

    def backward(chunk):
        grad_hidden = lax.dot_general(
            stacked(1, chunk), w_out[...], (((1,), (1,)), ((), ())), preferred_element_type=F32
        )
        value = (grad_hidden * slope[chunk]).astype(BF16)
        grad_pre[chunk] = value
        partial = lax.dot_general(
            value, w_in[...], (((1,), (1,)), ((), ())), preferred_element_type=F32
        )
        parts[chunk] = partial.astype(BF16).reshape(parts.shape[1:])

    cross_wait(0)
    mine[0][...] = compact(0).astype(BF16)
    spread_one(0)
    spread_two(0)
    spread_three(0)
    cross_wait(1)
    mine[1][...] = (gate_col * compact(1)).astype(BF16)
    spread_one(1)
    spread_four(0)
    spread_five(0)
    spread_two(1)
    loads[2].wait()
    forward(0)
    spread_three(1)
    forward(1)
    spread_four(1)
    forward(2)
    forward(3)
    spread_five(1)
    loads[3].wait()

    def unit(half, spot, begin=0, count=SIDE):
        rows = pl.ds(half * HALF, HALF)
        if half == 0:
            return parts.at[spot, pl.ds(begin, count), rows, :]
        return parts.at[pl.ds(begin, count), spot, rows, :]

    def tally(half, move):
        first, second = (spot_x, spot_y) if half == 0 else (spot_y, spot_x)
        close, through = near, passing
        if move == 0:
            way, source, target = 1, unit(half, wrap(first + 1)), close.at[half, 0]
        elif move == 1:
            way, source, target = -1, unit(half, wrap(first - 1)), close.at[half, 1]
        elif move == 2:
            way, source, target = 1, unit(half, wrap(first + 2), 0, 2), through.at[half, 0]
        elif move == 3:
            way, source, target = -1, unit(half, wrap(first + 2), 2, 2), through.at[half, 1]
        elif move == 4:
            way, source, target = 1, through.at[half, 0], close.at[half, 2, pl.ds(0, 2)]
        elif move == 5:
            way, source, target = -1, through.at[half, 1], close.at[half, 2, pl.ds(2, 2)]
        else:
            way = (1, -1, 2)[move - 6]
            source = summed.at[half, wrap(second + way)]
            target = last.at[half, move - 6]
        if move < 6:
            peer = place(half, wrap(first + way), second)
        else:
            peer = place(half, first, wrap(second + way))
        return pltpu.make_async_remote_copy(
            src_ref=source,
            dst_ref=target,
            send_sem=sum_send.at[half, move],
            recv_sem=sum_recv.at[half, move],
            device_id={"dp": peer},
            device_id_type=MESH,
        )

    def tally_relay():
        for half in halves:
            tally(half, 2).wait_recv()
            tally(half, 4).start()
            tally(half, 3).wait_recv()
            tally(half, 5).start()

    def tally_near():
        for half in halves:
            for move in (0, 1, 4, 5):
                tally(half, move).wait_recv()
            index = spot_x if half == 0 else spot_y
            rows = slice(half * HALF, half * HALF + HALF)
            for spot in range(SIDE):
                if half == 0:
                    own = parts[index, spot, rows, :]
                else:
                    own = parts[spot, index, rows, :]
                value = own.astype(F32)
                for source in range(3):
                    value = value + near[half, source, spot].astype(F32)
                summed[half, spot] = value.astype(BF16)
            for move in (8, 6, 7):
                tally(half, move).start()

    def give_back():
        totals = []
        for half in halves:
            for move in (6, 7, 8):
                tally(half, move).wait_recv()
            index = spot_y if half == 0 else spot_x
            value = summed[half, index].astype(F32)
            for source in range(3):
                value = value + last[half, source].astype(F32)
            totals.append(value.astype(BF16))
        total = jnp.concatenate(totals, axis=0)
        send[2][...] = turned(slot_hits, total).astype(BF16).reshape(send[2].shape)
        cross_start(2)

    backward(wrap(spot_x + 2))
    tally(0, 2).start()
    tally(0, 3).start()
    backward(wrap(spot_x + 1))
    tally(0, 0).start()
    backward(wrap(spot_x - 1))
    tally(0, 1).start()
    backward(spot_x)
    for move in (2, 3, 0, 1):
        tally(1, move).start()
    tally_relay()
    hidden_rows = hidden[...].reshape(SIDE * hidden.shape[1], hidden.shape[2])
    grad_rows = grad_pre[...].reshape(hidden_rows.shape)

    rows_grad = full[1][...].reshape(hidden_rows.shape[0], width)
    hold_wout[...] = turned(hidden_rows, rows_grad).astype(BF16)
    store_wout = pltpu.make_async_copy(hold_wout, out_wout, load_sem.at[4])
    store_wout.start()
    tally_near()
    give_back()
    for begin, count in ((0, CUT), (CUT, width - CUT)):
        rows_in = full[0][:, :, begin : begin + count].reshape(hidden_rows.shape[0], count)
        hold_win[begin : begin + count, :] = turned(rows_in, grad_rows).astype(BF16)
    store_win = pltpu.make_async_copy(hold_win, out_win, load_sem.at[5])
    store_win.start()
    for which in range(2):
        spread_sent(which)
    for half in halves:
        for move in range(9):
            tally(half, move).wait_send()
    cross_sent(0)
    cross_sent(1)
    cross_wait(2)
    cross_sent(2)
    store_wout.wait()
    store_win.wait()


def tail_kernel(
    picks, back, win_hbm, wout_hbm, out_patches, out_win, out_wout, win, wout, sem_in, sem_out
):
    width = out_patches.shape[1]
    loads, stores = [], []
    for i, (source, held, target) in enumerate(((win_hbm, win, out_win), (wout_hbm, wout, out_wout))):
        step = source.shape[0] // 2
        for half in range(2):
            rows = pl.ds(half * step, step)
            at = 2 * i + half
            loads.append(pltpu.make_async_copy(source.at[rows], held.at[rows], sem_in.at[at]))
            stores.append(pltpu.make_async_copy(held.at[rows], target.at[rows], sem_out.at[at]))
    for load in loads:
        load.start()
    owner_hits = pick_table(picks, out_patches.shape[0])
    rows = back[...].reshape(back.shape[0] * back.shape[1], width)
    out_patches[...] = jnp.dot(owner_hits, rows, preferred_element_type=F32).astype(BF16)
    for load, store in zip(loads, stores):
        load.wait()
        store.start()
    for store in stores:
        store.wait()


def on_device(patches, grad_out, weight_in, weight_out, gates, counts, picks):
    tokens = patches.shape[2]
    width = patches.shape[3]
    experts = picks.shape[2]
    ranks = picks.shape[3]
    groups = counts.shape[0]
    capacity = gates.shape[2]
    units = weight_in.shape[2]
    side_rows = groups * capacity // SIDE
    in_vmem = pl.BlockSpec(memory_space=pltpu.VMEM)
    in_place = pl.BlockSpec(memory_space=pl.ANY)
    shape_in = jax.ShapeDtypeStruct((width, units), BF16)
    shape_out = jax.ShapeDtypeStruct((units, width), BF16)
    local_picks = jnp.transpose(picks[0, 0])
    slab = (experts, ranks, width)
    back, grad_in, grad_out_weight = pl.pallas_call(
        layer_kernel,
        out_shape=[jax.ShapeDtypeStruct(slab, BF16), shape_in, shape_out],
        in_specs=[in_place] * 4 + [in_vmem] * 3,
        out_specs=[in_vmem] + [in_place] * 2,
        scratch_shapes=[
            pltpu.VMEM((tokens, width), BF16),
            pltpu.VMEM((tokens, width), BF16),
            pltpu.VMEM((width, units), BF16),
            pltpu.VMEM((units, width), BF16),
            pltpu.VMEM((width, units), BF16),
            pltpu.VMEM((units, width), BF16),
        ]
        + [pltpu.VMEM(slab, BF16)] * 5
        + [pltpu.VMEM((capacity, width), BF16)] * 2
        + [pltpu.VMEM((groups, capacity, width), BF16)] * 2
        + [
            pltpu.VMEM((SIDE, side_rows, units), BF16),
            pltpu.VMEM((SIDE, side_rows, units), F32),
            pltpu.VMEM((SIDE, side_rows, units), BF16),
            pltpu.VMEM((SIDE, SIDE, capacity, width), BF16),
            pltpu.VMEM((2, 3, SIDE, HALF, width), BF16),
            pltpu.VMEM((2, 2, 2, HALF, width), BF16),
            pltpu.VMEM((2, SIDE, HALF, width), BF16),
            pltpu.VMEM((2, 3, HALF, width), BF16),
            pltpu.SemaphoreType.DMA((6,)),
            pltpu.SemaphoreType.DMA((5,)),
            pltpu.SemaphoreType.DMA((3, experts)),
            pltpu.SemaphoreType.DMA((3, experts)),
            pltpu.SemaphoreType.DMA((2, 2, 5, 4)),
            pltpu.SemaphoreType.DMA((2, 2, 5, 4)),
            pltpu.SemaphoreType.DMA((2, 9)),
            pltpu.SemaphoreType.DMA((2, 9)),
        ],
        compiler_params=pltpu.CompilerParams(
            collective_id=1, has_side_effects=True, vmem_limit_bytes=56 * 1024 * 1024
        ),
    )(
        patches[0, 0],
        grad_out[0, 0],
        weight_in[0],
        weight_out[0],
        gates[0],
        jnp.transpose(counts, (0, 2, 1)),
        local_picks,
    )
    grad_patches, grad_in, grad_out_weight = pl.pallas_call(
        tail_kernel,
        out_shape=[jax.ShapeDtypeStruct((tokens, width), BF16), shape_in, shape_out],
        in_specs=[in_vmem] * 2 + [in_place] * 2,
        out_specs=[in_vmem] + [in_place] * 2,
        scratch_shapes=[
            pltpu.VMEM((width, units), BF16),
            pltpu.VMEM((units, width), BF16),
            pltpu.SemaphoreType.DMA((4,)),
            pltpu.SemaphoreType.DMA((4,)),
        ],
        compiler_params=pltpu.CompilerParams(vmem_limit_bytes=56 * 1024 * 1024),
    )(local_picks, back, grad_in, grad_out_weight)
    return (grad_patches[None, None], grad_in[None], grad_out_weight[None])


def solution(mesh):
    return jax.shard_map(
        on_device,
        mesh=mesh,
        in_specs=(
            P("dp", "expert", None, None),
            P("dp", "expert", None, None),
            P("expert", None, "dp"),
            P("expert", "dp", None),
            P("expert", "dp", None),
            P(None, None, "expert"),
            P("dp", "expert", None, None),
        ),
        out_specs=(P("dp", "expert", None, None), P("expert", None, "dp"), P("expert", "dp", None)),
        check_vma=False,
    )
```

```python
import jax
import jax.numpy as jnp
from jax import lax
from jax.experimental import pallas as pl
from jax.experimental.pallas import tpu as pltpu
from jax.sharding import PartitionSpec as P

MESH = pl.DeviceIdType.MESH
SIDE = 4
HALF = 16
CUT = 896
BF16 = jnp.bfloat16
F32 = jnp.float32

gelu_scale = 0.7978845608028654
gelu_cubic = 0.044715


def gelu_parts(preact):
    inner_arg = gelu_scale * (preact + gelu_cubic * preact * preact * preact)
    tangent = jnp.tanh(inner_arg)
    gelu_value = 0.5 * preact * (1.0 + tangent)
    gelu_slope = 0.5 * (1.0 + tangent) + 0.5 * preact * (1.0 - tangent * tangent) * gelu_scale * (
        1.0 + 3.0 * gelu_cubic * preact * preact
    )
    return (gelu_value, gelu_slope)


def wrap(value):
    return lax.rem(value + 2 * SIDE, SIDE)


def place(half, first, second):
    return first * SIDE + second if half == 0 else second * SIDE + first


def widths_of(width):
    return ((0, width), (0, width))


def pick_table(picks, tokens):
    ranks, experts = picks.shape
    total = ranks * experts
    owner = lax.broadcasted_iota(jnp.int32, (experts, total), 0)
    entry = lax.broadcasted_iota(jnp.int32, (experts, total), 1)
    row = jnp.zeros((1, total), F32)
    for rank in range(ranks):
        spread_out = (entry == ranks * owner + rank).astype(BF16)
        values = picks[rank : rank + 1, :].astype(F32).astype(BF16)
        row = row + jnp.dot(values, spread_out, preferred_element_type=F32)
    token = lax.broadcasted_iota(jnp.int32, (tokens, total), 0)
    return (token == row.astype(jnp.int32)).astype(BF16)


def slot_table(counts, capacity, ranks):
    owners = counts.shape[1]
    total = ranks * owners
    owner = lax.broadcasted_iota(jnp.int32, (owners, total), 0)
    entry = lax.broadcasted_iota(jnp.int32, (owners, total), 1)
    before = (ranks * owner + ranks <= entry).astype(BF16)
    here = ((ranks * owner <= entry) & (entry < ranks * owner + ranks)).astype(BF16)
    taken = counts.astype(F32).astype(BF16)
    begin = jnp.dot(taken, before, preferred_element_type=F32)
    count = jnp.dot(taken, here, preferred_element_type=F32)
    rank = lax.rem(lax.broadcasted_iota(jnp.int32, (1, total), 1), ranks).astype(F32)
    slot = jnp.where(rank < count, begin + rank, -1.0).astype(jnp.int32)
    row = lax.broadcasted_iota(jnp.int32, (capacity, total), 0)
    return (row == slot).astype(BF16)


def layer_kernel(*refs):
    (patches_hbm, grad_hbm, win_hbm, wout_hbm, gates, counts, picks) = refs[:7]
    back = refs[7:8]
    out_win, out_wout = refs[8:10]
    (patches, grads, w_in, w_out, hold_win, hold_wout) = refs[10:16]
    send = refs[16:19]
    recv = refs[19:21] + back
    mine = refs[21:23]
    full = refs[23:25]
    (hidden, slope, grad_pre, parts, near, passing, summed, last) = refs[25:33]
    (load_sem, own_sem, cross_send, cross_recv) = refs[33:37]
    (spread_send, spread_recv, sum_send, sum_recv) = refs[37:]
    experts, ranks = send[0].shape[:2]
    capacity = mine[0].shape[0]
    width = patches.shape[1]
    spans = widths_of(width)
    me = lax.axis_index("expert")
    group = lax.axis_index("dp")
    spot_x, spot_y = lax.div(group, SIDE), lax.rem(group, SIDE)
    barrier = pltpu.get_barrier_semaphore()

    def offset_of(step):
        sign = 1 - 2 * lax.rem(step, 2)
        return experts // 2 + sign * lax.div(step + 1, 2)

    def greet(step, carry):
        peer = lax.rem(me + offset_of(step), experts)
        pl.semaphore_signal(barrier, inc=1, device_id={"expert": peer}, device_id_type=MESH)
        return carry

    lax.fori_loop(0, experts - 1, greet, 0)
    for shift in (1, -1, 2):
        for half in range(2):
            first, second = (spot_x, spot_y) if half == 0 else (spot_y, spot_x)
            pl.semaphore_signal(
                barrier,
                inc=1,
                device_id={"dp": place(half, wrap(first + shift), second)},
                device_id_type=MESH,
            )

    loads = [
        pltpu.make_async_copy(source, target, load_sem.at[i])
        for i, (source, target) in enumerate(
            ((patches_hbm, patches), (grad_hbm, grads), (win_hbm, w_in), (wout_hbm, w_out))
        )
    ]
    for load in loads:
        load.start()

    def cross(i, step, incoming):
        offset = offset_of(step)
        peer = lax.rem(me + (experts - offset if incoming else offset), experts)
        return pltpu.make_async_remote_copy(
            src_ref=send[i].at[peer],
            dst_ref=recv[i].at[peer if incoming else me],
            send_sem=cross_send.at[i, offset],
            recv_sem=cross_recv.at[i, offset],
            device_id={"expert": peer},
            device_id_type=MESH,
        )

    def own_block(i):
        return pltpu.make_async_copy(send[i].at[me], recv[i].at[me], own_sem.at[i])

    def cross_start(i, begin=0, end=experts - 1):
        def launch(step, carry):
            cross(i, step, False).start()
            return carry

        lax.fori_loop(begin, end, launch, 0)
        if begin == 0:
            own_block(i).start()

    def cross_wait(i):
        def finish(step, carry):
            cross(i, step, True).wait_recv()
            return carry

        lax.fori_loop(0, experts - 1, finish, 0)
        own_block(i).wait()

    def cross_sent(i):
        def finish(step, carry):
            cross(i, step, False).wait_send()
            return carry

        lax.fori_loop(0, experts - 1, finish, 0)

    pick_hits = pick_table(picks, patches.shape[0])
    slot_hits = slot_table(counts[group], capacity, ranks)
    diagonal = lax.broadcasted_iota(jnp.int32, (capacity, capacity), 0) == (
        lax.broadcasted_iota(jnp.int32, (capacity, capacity), 1)
    )
    gate_col = jnp.sum(jnp.where(diagonal, gates[...], 0.0), axis=1, keepdims=True)

    def turned(left, right):
        return lax.dot_general(left, right, (((0,), (0,)), ((), ())), preferred_element_type=F32)

    loads[0].wait()
    send[0][...] = turned(pick_hits, patches[...]).astype(BF16).reshape(send[0].shape)
    loads[1].wait()
    send[1][...] = turned(pick_hits, grads[...]).astype(BF16).reshape(send[1].shape)
    pl.semaphore_wait(barrier, experts - 1 + 6)
    cross_start(0)
    cross_start(1)

    def compact(i):
        rows = recv[i][...].reshape(ranks * experts, spans[i][1])
        return jnp.dot(slot_hits, rows, preferred_element_type=F32)

    def piece(which, half, stage, move, incoming):
        way = (1, -1, 1, -1)[move]
        first, second = (spot_x, spot_y) if half == 0 else (spot_y, spot_x)
        rows = pl.ds(half * HALF, HALF)
        wide = spans[which][1]
        split = (wide // 256 + 1) * 128 if wide % 256 else wide // 2
        columns = (pl.ds(0, wide), pl.ds(0, wide), pl.ds(0, split), pl.ds(split, wide - split))[
            move
        ]
        back_by = (0 if move < 2 else -way) - (way if incoming else 0)
        if stage == 0:
            block = place(half, wrap(first + back_by), second)
            peer = place(half, wrap(first + way), second)
        else:
            held = wrap(first + (0, -1, 1, 2)[stage - 1])
            block = place(half, held, wrap(second + back_by))
            peer = place(half, first, wrap(second + way))
        target = full[which].at[block, rows, columns]
        source = target
        if not incoming and move < 2 and stage < 2:
            source = mine[which].at[rows, columns]
        return pltpu.make_async_remote_copy(
            src_ref=source,
            dst_ref=target,
            send_sem=spread_send.at[which, half, stage, move],
            recv_sem=spread_recv.at[which, half, stage, move],
            device_id={"dp": peer},
            device_id_type=MESH,
        )

    def launch(which, half, stage, *moves):
        for move in moves:
            piece(which, half, stage, move, False).start()

    def arrive(which, half, stage, move):
        piece(which, half, stage, move, True).wait_recv()

    def relay(which, half, stage):
        arrive(which, half, stage, 0)
        launch(which, half, stage, 2)
        arrive(which, half, stage, 1)
        launch(which, half, stage, 3)

    def own_rows(which):
        return pltpu.make_async_copy(mine[which], full[which].at[group], own_sem.at[3 + which])

    halves = range(2)

    def spread_one(which):
        for stage in (0, 1):
            for half in halves:
                launch(which, half, stage, 0, 1)
        own_rows(which).start()

    def spread_two(which):
        for half in halves:
            arrive(which, half, 0, 0)
            launch(which, half, 0, 2)
            launch(which, half, 2, 0, 1)
            arrive(which, half, 0, 1)
            launch(which, half, 0, 3)
            launch(which, half, 3, 0, 1)

    def spread_three(which):
        for half in halves:
            relay(which, half, 1)
        for half in halves:
            arrive(which, half, 0, 2)
            arrive(which, half, 0, 3)
            launch(which, half, 4, 0, 1)

    def spread_four(which):
        for stage in (2, 3, 4):
            for half in halves:
                relay(which, half, stage)

    def spread_five(which):
        for stage in (1, 2, 3, 4):
            for half in halves:
                arrive(which, half, stage, 2)
                arrive(which, half, stage, 3)
        own_rows(which).wait()

    def spread_sent(which):
        for stage in range(5):
            for half in halves:
                for move in range(4):
                    piece(which, half, stage, move, False).wait_send()

    def stacked(which, chunk):
        rows = full[which][pl.ds(SIDE * chunk, SIDE)]
        return rows.reshape(SIDE * capacity, spans[which][1])

    def forward(chunk):
        preact = jnp.dot(stacked(0, chunk), w_in[...], preferred_element_type=F32)
        gelu_value, gelu_slope = gelu_parts(preact)
        hidden[chunk] = gelu_value.astype(BF16)
        slope[chunk] = gelu_slope

    def backward(chunk):
        grad_hidden = lax.dot_general(
            stacked(1, chunk), w_out[...], (((1,), (1,)), ((), ())), preferred_element_type=F32
        )
        value = (grad_hidden * slope[chunk]).astype(BF16)
        grad_pre[chunk] = value
        partial = lax.dot_general(
            value, w_in[...], (((1,), (1,)), ((), ())), preferred_element_type=F32
        )
        parts[chunk] = partial.astype(BF16).reshape(parts.shape[1:])

    cross_wait(0)
    mine[0][...] = compact(0).astype(BF16)
    spread_one(0)
    spread_two(0)
    spread_three(0)
    cross_wait(1)
    mine[1][...] = (gate_col * compact(1)).astype(BF16)
    spread_one(1)
    spread_four(0)
    spread_two(1)
    spread_five(0)
    loads[2].wait()
    spread_three(1)
    forward(0)
    spread_four(1)
    forward(1)
    forward(2)
    forward(3)
    spread_five(1)
    loads[3].wait()

    def unit(half, spot, begin=0, count=SIDE):
        rows = pl.ds(half * HALF, HALF)
        if half == 0:
            return parts.at[spot, pl.ds(begin, count), rows, :]
        return parts.at[pl.ds(begin, count), spot, rows, :]

    def tally(half, move):
        first, second = (spot_x, spot_y) if half == 0 else (spot_y, spot_x)
        close, through = near, passing
        if move == 0:
            way, source, target = 1, unit(half, wrap(first + 1)), close.at[half, 0]
        elif move == 1:
            way, source, target = -1, unit(half, wrap(first - 1)), close.at[half, 1]
        elif move == 2:
            way, source, target = 1, unit(half, wrap(first + 2), 0, 2), through.at[half, 0]
        elif move == 3:
            way, source, target = -1, unit(half, wrap(first + 2), 2, 2), through.at[half, 1]
        elif move == 4:
            way, source, target = 1, through.at[half, 0], close.at[half, 2, pl.ds(0, 2)]
        elif move == 5:
            way, source, target = -1, through.at[half, 1], close.at[half, 2, pl.ds(2, 2)]
        else:
            way = (1, -1, 2)[move - 6]
            source = summed.at[half, wrap(second + way)]
            target = last.at[half, move - 6]
        if move < 6:
            peer = place(half, wrap(first + way), second)
        else:
            peer = place(half, first, wrap(second + way))
        return pltpu.make_async_remote_copy(
            src_ref=source,
            dst_ref=target,
            send_sem=sum_send.at[half, move],
            recv_sem=sum_recv.at[half, move],
            device_id={"dp": peer},
            device_id_type=MESH,
        )

    def tally_relay():
        for half in halves:
            tally(half, 2).wait_recv()
            tally(half, 4).start()
            tally(half, 3).wait_recv()
            tally(half, 5).start()

    def tally_near():
        for half in halves:
            for move in (0, 1, 4, 5):
                tally(half, move).wait_recv()
            index = spot_x if half == 0 else spot_y
            rows = slice(half * HALF, half * HALF + HALF)
            for spot in range(SIDE):
                if half == 0:
                    own = parts[index, spot, rows, :]
                else:
                    own = parts[spot, index, rows, :]
                value = own.astype(F32)
                for source in range(3):
                    value = value + near[half, source, spot].astype(F32)
                summed[half, spot] = value.astype(BF16)
            for move in (8, 6, 7):
                tally(half, move).start()

    def give_back():
        totals = []
        for half in halves:
            for move in (6, 7, 8):
                tally(half, move).wait_recv()
            index = spot_y if half == 0 else spot_x
            value = summed[half, index].astype(F32)
            for source in range(3):
                value = value + last[half, source].astype(F32)
            totals.append(value.astype(BF16))
        total = jnp.concatenate(totals, axis=0)
        send[2][...] = turned(slot_hits, total).astype(BF16).reshape(send[2].shape)
        cross_start(2)

    backward(wrap(spot_x + 2))
    tally(0, 2).start()
    tally(0, 3).start()
    backward(wrap(spot_x + 1))
    tally(0, 0).start()
    backward(wrap(spot_x - 1))
    tally(0, 1).start()
    backward(spot_x)
    for move in (2, 3, 0, 1):
        tally(1, move).start()
    tally_relay()
    hidden_rows = hidden[...].reshape(SIDE * hidden.shape[1], hidden.shape[2])
    grad_rows = grad_pre[...].reshape(hidden_rows.shape)

    rows_grad = full[1][...].reshape(hidden_rows.shape[0], width)
    hold_wout[...] = turned(hidden_rows, rows_grad).astype(BF16)
    store_wout = pltpu.make_async_copy(hold_wout, out_wout, load_sem.at[4])
    store_wout.start()
    tally_near()
    give_back()
    for begin, count in ((0, CUT), (CUT, width - CUT)):
        rows_in = full[0][:, :, begin : begin + count].reshape(hidden_rows.shape[0], count)
        hold_win[begin : begin + count, :] = turned(rows_in, grad_rows).astype(BF16)
    store_win = pltpu.make_async_copy(hold_win, out_win, load_sem.at[5])
    store_win.start()
    for which in range(2):
        spread_sent(which)
    for half in halves:
        for move in range(9):
            tally(half, move).wait_send()
    cross_sent(0)
    cross_sent(1)
    cross_wait(2)
    cross_sent(2)
    store_wout.wait()
    store_win.wait()


def tail_kernel(
    picks, back, win_hbm, wout_hbm, out_patches, out_win, out_wout, win, wout, sem_in, sem_out
):
    width = out_patches.shape[1]
    loads, stores = [], []
    for i, (source, held, target) in enumerate(((win_hbm, win, out_win), (wout_hbm, wout, out_wout))):
        step = source.shape[0] // 2
        for half in range(2):
            rows = pl.ds(half * step, step)
            at = 2 * i + half
            loads.append(pltpu.make_async_copy(source.at[rows], held.at[rows], sem_in.at[at]))
            stores.append(pltpu.make_async_copy(held.at[rows], target.at[rows], sem_out.at[at]))
    for load in loads:
        load.start()
    owner_hits = pick_table(picks, out_patches.shape[0])
    rows = back[...].reshape(back.shape[0] * back.shape[1], width)
    out_patches[...] = jnp.dot(owner_hits, rows, preferred_element_type=F32).astype(BF16)
    for load, store in zip(loads, stores):
        load.wait()
        store.start()
    for store in stores:
        store.wait()


def on_device(patches, grad_out, weight_in, weight_out, gates, counts, picks):
    tokens = patches.shape[2]
    width = patches.shape[3]
    experts = picks.shape[2]
    ranks = picks.shape[3]
    groups = counts.shape[0]
    capacity = gates.shape[2]
    units = weight_in.shape[2]
    side_rows = groups * capacity // SIDE
    in_vmem = pl.BlockSpec(memory_space=pltpu.VMEM)
    in_place = pl.BlockSpec(memory_space=pl.ANY)
    shape_in = jax.ShapeDtypeStruct((width, units), BF16)
    shape_out = jax.ShapeDtypeStruct((units, width), BF16)
    local_picks = jnp.transpose(picks[0, 0])
    slab = (experts, ranks, width)
    back, grad_in, grad_out_weight = pl.pallas_call(
        layer_kernel,
        out_shape=[jax.ShapeDtypeStruct(slab, BF16), shape_in, shape_out],
        in_specs=[in_place] * 4 + [in_vmem] * 3,
        out_specs=[in_vmem] + [in_place] * 2,
        scratch_shapes=[
            pltpu.VMEM((tokens, width), BF16),
            pltpu.VMEM((tokens, width), BF16),
            pltpu.VMEM((width, units), BF16),
            pltpu.VMEM((units, width), BF16),
            pltpu.VMEM((width, units), BF16),
            pltpu.VMEM((units, width), BF16),
        ]
        + [pltpu.VMEM(slab, BF16)] * 5
        + [pltpu.VMEM((capacity, width), BF16)] * 2
        + [pltpu.VMEM((groups, capacity, width), BF16)] * 2
        + [
            pltpu.VMEM((SIDE, side_rows, units), BF16),
            pltpu.VMEM((SIDE, side_rows, units), F32),
            pltpu.VMEM((SIDE, side_rows, units), BF16),
            pltpu.VMEM((SIDE, SIDE, capacity, width), BF16),
            pltpu.VMEM((2, 3, SIDE, HALF, width), BF16),
            pltpu.VMEM((2, 2, 2, HALF, width), BF16),
            pltpu.VMEM((2, SIDE, HALF, width), BF16),
            pltpu.VMEM((2, 3, HALF, width), BF16),
            pltpu.SemaphoreType.DMA((6,)),
            pltpu.SemaphoreType.DMA((5,)),
            pltpu.SemaphoreType.DMA((3, experts)),
            pltpu.SemaphoreType.DMA((3, experts)),
            pltpu.SemaphoreType.DMA((2, 2, 5, 4)),
            pltpu.SemaphoreType.DMA((2, 2, 5, 4)),
            pltpu.SemaphoreType.DMA((2, 9)),
            pltpu.SemaphoreType.DMA((2, 9)),
        ],
        compiler_params=pltpu.CompilerParams(
            collective_id=1, has_side_effects=True, vmem_limit_bytes=56 * 1024 * 1024
        ),
    )(
        patches[0, 0],
        grad_out[0, 0],
        weight_in[0],
        weight_out[0],
        gates[0],
        jnp.transpose(counts, (0, 2, 1)),
        local_picks,
    )
    grad_patches, grad_in, grad_out_weight = pl.pallas_call(
        tail_kernel,
        out_shape=[jax.ShapeDtypeStruct((tokens, width), BF16), shape_in, shape_out],
        in_specs=[in_vmem] * 2 + [in_place] * 2,
        out_specs=[in_vmem] + [in_place] * 2,
        scratch_shapes=[
            pltpu.VMEM((width, units), BF16),
            pltpu.VMEM((units, width), BF16),
            pltpu.SemaphoreType.DMA((4,)),
            pltpu.SemaphoreType.DMA((4,)),
        ],
        compiler_params=pltpu.CompilerParams(vmem_limit_bytes=56 * 1024 * 1024),
    )(local_picks, back, grad_in, grad_out_weight)
    return (grad_patches[None, None], grad_in[None], grad_out_weight[None])


def solution(mesh):
    return jax.shard_map(
        on_device,
        mesh=mesh,
        in_specs=(
            P("dp", "expert", None, None),
            P("dp", "expert", None, None),
            P("expert", None, "dp"),
            P("expert", "dp", None),
            P("expert", "dp", None),
            P(None, None, "expert"),
            P("dp", "expert", None, None),
        ),
        out_specs=(P("dp", "expert", None, None), P("expert", None, "dp"), P("expert", "dp", None)),
        check_vma=False,
    )
```
